256 devices in a mesh: gx: 8 (over z), gz: 8 (over y, core), row: 4 (over x).
Axes of the slice: x: 4, y: 4, z: 8, core: 2. Of those that a mesh axis runs over, the one named last changes fastest.
Arguments:
- flow_field: float32 [5, 32, 256, 512], P(None, 'gx', 'gz', 'row'), may hold values from -6 to 6
- flux_jacobian: float32 [3, 5, 5], replicated, may hold values from -2.5 to 2.5
- history: float32 [98304, 5, 128], P(('gx', 'gz', 'row')), may hold values from -6 to 6
- surface_cell: int32 [1536, 64], P(('gx', 'gz', 'row')), may hold values from 0 to 16383
- surface_blocks: int32 [4, 64], P('row', ('gx', 'gz')), may hold values from 1 to 6, 128 in all within a row
- observers: float32 [3, 256], replicated, may hold values from 0 to 1
Outputs:
- field_out: float32 [5, 32, 256, 512], P(None, 'gx', 'gz', 'row')
- spectrum: float32 [256, 64], P(('gx', 'gz', 'row'))
The draws below stay inside these ranges and needn't reach their ends.
Inputs may be any that keep to these rules, and one draw needn't show every extreme that they name: The patch with index g of gx+gz and index q of row has exactly 64 * surface_blocks[q, g] live slots, its first ones.
All inputs are finite; a program needn't handle non-finite values. No bound on the sum of `surface_blocks` on one device may be relied on, other than what follows from the above.
Results may differ from the reference program's by a relative error of at most 0.0003.
Values sent between devices are 32-bit elements; how exact they have to be, the bound alone decides.
A program may use at most 64 MiB of HBM per device.

```python
import math
import jax
import jax.numpy as jnp
import numpy as np
from jax import lax

CX = 4
CZ = 32
CR = 128
SURF_DEV = 128
NT = 128
FREQ = 32
OBS = 256
STEPS = 3
OWNERS = 64
SLOT = 6
SP_CAP = 384
NX = 32
NZ = 256
NR = 512
N_GX = 8
N_GZ = 8
N_ROW = 4
DEVICES = 256


def plant(array, rng, low, high):
    longest = array.shape.index(max(array.shape))
    spots = []
    for shift in (0, 1):
        where = [jax.random.randint(jax.random.fold_in(rng, axis), (), 0, length) for axis, length in enumerate(array.shape)]
        where[longest] = (where[longest] + shift) % array.shape[longest]
        spots.append(tuple(where))
    return array.at[spots[0]].set(low).at[spots[1]].set(high)


def steps_of(own_key, extent, pieces, least, top_value):
    loudness = 1.0
    for position, blocks in pieces:
        draws = jax.random.uniform(jax.random.fold_in(jax.random.fold_in(own_key, 6), position), (blocks,), jnp.float32, least / len(pieces), top_value / len(pieces))
        loudness = loudness * jnp.repeat(jnp.exp(draws), extent[position] // blocks).reshape((-1,) + (1,) * (len(extent) - 1 - position))
    return loudness


def profile(amount, total, limit, lean):
    loads = [(1 << 20) // math.isqrt(grade ** lean) + 1 for grade in range(2, amount + 1)]
    surplus, holding = total - limit - (amount - 1), [1] * (amount - 1)
    while surplus > 0:
        candidates = [i for i in range(amount - 1) if holding[i] < limit]
        mass, budget = sum([loads[i] for i in candidates]), surplus
        for i in candidates:
            extra = min(limit - holding[i], max(1, budget * loads[i] // mass), surplus)
            holding[i] = holding[i] + extra
            surplus = surplus - extra
    return np.array([limit] + holding)


def uneven_parts(stream_key, number_of, total, most, slope):
    if number_of == 2:
        one = jax.random.randint(stream_key, (), max(1, total - most), min(most, total - 1) + 1)
        return jnp.stack([one, total - one])
    tallies = jnp.asarray(profile(number_of, total, most, slope), jnp.int32)
    twos = (number_of - 1) // 2
    giver, sink = tallies[1:1 + 2 * twos:2], tallies[2:2 + 2 * twos:2]
    slack = jnp.minimum(giver - 1, most - sink)
    passed = jax.random.randint(jax.random.fold_in(stream_key, 1), (twos,), 0, 1 << 20) % (slack + 1)
    tallies = tallies.at[1:1 + 2 * twos:2].set(giver - passed).at[2:2 + 2 * twos:2].set(sink + passed)
    return tallies[jax.random.permutation(jax.random.fold_in(stream_key, 2), number_of)]


def gaussian(key, extent, spread, most, pieces=(), held_as=jnp.bfloat16):
    result = jax.random.normal(key, extent, jnp.float32) * spread
    if len(pieces) > 0:
        result = steps_of(key, extent, pieces, -0.22, 0.18) * result
    return jnp.clip(result, min=-most, max=most).astype(held_as)


def setup_inputs(seed: int = 0) -> dict:
    keys = jax.random.split(jax.random.key(seed), 7)
    return {
        "flow_field": gaussian(keys[0], (5, NX, NZ, NR), 1.0, 6.0, ((1, 8), (2, 8), (3, 4)), jnp.float32),
        "flux_jacobian": gaussian(keys[1], (3, 5, 5), 5 ** -0.5, 2.5, (), jnp.float32),
        "history": gaussian(keys[2], (DEVICES * SP_CAP, 5, NT), 1.0, 6.0, ((0, 256),), jnp.float32),
        "surface_cell": plant(jax.random.randint(keys[3], (DEVICES * SLOT, OWNERS), 0, CX * CZ * CR), jax.random.fold_in(keys[3], 1), 0, (CX * CZ * CR) - 1).astype(jnp.int32),
        "surface_blocks": jax.vmap(lambda own: uneven_parts(own, OWNERS, SURF_DEV, SLOT, 2))(jax.random.split(keys[4], N_ROW)).reshape((N_ROW, OWNERS)).astype(jnp.int32),
        "observers": jnp.clip(jax.random.uniform(keys[5], (3, OBS), jnp.float32, 0.0, 1.0), 0.0, 1.0),
    }


TIME_STEP = 0.3
VISCOSITY = 0.05

def stencil_rate(padded, flux_jacobian):
    center = padded[:, 1:-1, 1:-1, 1:-1]
    along_x = (padded[:, 2:, 1:-1, 1:-1] - padded[:, :-2, 1:-1, 1:-1]) * 0.5
    along_z = (padded[:, 1:-1, 2:, 1:-1] - padded[:, 1:-1, :-2, 1:-1]) * 0.5
    along_r = (padded[:, 1:-1, 1:-1, 2:] - padded[:, 1:-1, 1:-1, :-2]) * 0.5
    beside = padded[:, 2:, 1:-1, 1:-1] + padded[:, :-2, 1:-1, 1:-1]
    beside = beside + padded[:, 1:-1, 2:, 1:-1] + padded[:, 1:-1, :-2, 1:-1]
    beside = beside + padded[:, 1:-1, 1:-1, 2:] + padded[:, 1:-1, 1:-1, :-2]
    slopes = jnp.stack([along_x, along_z, along_r])
    transport = jnp.einsum('dvw,dwxzr->vxzr', flux_jacobian, slopes, precision=lax.Precision.HIGHEST)
    return transport + VISCOSITY * (beside - 6.0 * center)

def advance(current, rate_of):
    section_one = current + TIME_STEP * rate_of(current)
    section_two = 0.75 * current + 0.25 * (section_one + TIME_STEP * rate_of(section_one))
    return current / 3.0 + 2.0 / 3.0 * (section_two + TIME_STEP * rate_of(section_two))

def fourier_table(samples, freq_count):
    time_ids = jnp.arange(samples, dtype=jnp.int32)
    freq_ids = jnp.arange(1, freq_count + 1, dtype=jnp.int32)
    turn_ids = freq_ids[:, None] * time_ids[None, :] % samples
    angles = 2.0 * math.pi / samples * turn_ids.astype(jnp.float32)
    norm_scale = 1.0 / math.sqrt(samples)
    return jnp.concatenate([jnp.cos(angles), -jnp.sin(angles)], axis=0) * norm_scale

def spectra_of(signals, fourier):
    return jnp.einsum('ft,svt->vfs', fourier, signals, precision=lax.Precision.HIGHEST)

def radiate(points, monopole, dipole, watchers, radial_cells, freq_count):
    wavenumbers = jnp.arange(1, freq_count + 1, dtype=jnp.float32) * (2.0 / radial_cells)
    offset_vec = watchers[:, :, None] - points[None, :, :]
    distance = jnp.sqrt(lax.optimization_barrier(jnp.sum(offset_vec * offset_vec, axis=1)))
    direction = offset_vec / distance[:, None, :]
    amplitude = (radial_cells / distance)[:, None, :]
    dip_real = direction[:, 0, None, :] * dipole[0, None, :freq_count, :]
    dip_real = dip_real + direction[:, 1, None, :] * dipole[1, None, :freq_count, :]
    dip_real = dip_real + direction[:, 2, None, :] * dipole[2, None, :freq_count, :]
    dip_imag = direction[:, 0, None, :] * dipole[0, None, freq_count:, :]
    dip_imag = dip_imag + direction[:, 1, None, :] * dipole[1, None, freq_count:, :]
    dip_imag = dip_imag + direction[:, 2, None, :] * dipole[2, None, freq_count:, :]
    mono_real = monopole[None, :freq_count, :]
    mono_imag = monopole[None, freq_count:, :]
    phase_arg = distance[:, None, :] * wavenumbers[None, :, None]
    near_term = 1.0 / phase_arg
    cosine = amplitude * jnp.cos(phase_arg)
    sine = amplitude * jnp.sin(phase_arg)
    plus_weight = cosine * near_term + sine
    minus_weight = cosine - sine * near_term
    out_real = lax.optimization_barrier(jnp.sum(plus_weight * dip_real - minus_weight * dip_imag + sine * mono_real - cosine * mono_imag, axis=2))
    out_imag = lax.optimization_barrier(jnp.sum(minus_weight * dip_real + plus_weight * dip_imag + cosine * mono_real + sine * mono_imag, axis=2))
    return jnp.concatenate([out_real, out_imag], axis=1)

def reference(flow_field, flux_jacobian, history, surface_cell, surface_blocks, observers):
    padding = ((0, 0), (1, 1), (1, 1), (1, 1))

    def rate_of(values):
        return stencil_rate(jnp.pad(values, padding), flux_jacobian)
    owners = N_GX * N_GZ
    capacity = SLOT * owners
    cell_ids = surface_cell.reshape(-1)
    slot_ids = jnp.arange(DEVICES * capacity, dtype=jnp.int32)
    device = slot_ids // capacity
    local_slot = slot_ids % capacity
    index_x = device // (N_GZ * N_ROW)
    index_z = device // N_ROW % N_GZ
    index_r = device % N_ROW
    global_x = index_x * CX + cell_ids // (CZ * CR)
    global_z = index_z * CZ + cell_ids // CR % CZ
    global_r = index_r * CR + cell_ids % CR
    flat_index = ((global_x * NZ + global_z) * NR + global_r).astype(jnp.int32)
    current = flow_field
    sampled = []
    for step_index in range(STEPS):
        current = advance(current, rate_of)
        sampled.append(jnp.take(current.reshape(5, -1), flat_index, axis=1))
    live_limit = surface_blocks[index_r, index_x * N_GZ + index_z]
    is_live = local_slot // owners < live_limit
    chosen = jnp.nonzero(is_live, size=DEVICES * SURF_DEV)[0].astype(jnp.int32)
    recent = jnp.stack(sampled, axis=2)[:, chosen, :]
    signals = jnp.concatenate([history[chosen][:, :, :NT - STEPS], jnp.transpose(recent, (1, 0, 2))], axis=2)
    points = jnp.stack([global_x, global_z, global_r])[:, chosen].astype(jnp.float32) + 0.5
    spectra = spectra_of(signals, fourier_table(NT, FREQ))
    monopole = spectra[0] + spectra[4]
    dipole = spectra[1:4]
    watchers = jnp.stack([observers[0] * NX, observers[1] * NZ, (1.25 + 0.75 * observers[2]) * NR], axis=1)

    def one_block(block):
        return radiate(points, monopole, dipole, block, NR, FREQ)
    blocks_out = lax.map(one_block, watchers.reshape(OBS // 8, 8, 3))
    spectrum = blocks_out.reshape(OBS, 2 * FREQ) / math.sqrt(DEVICES * SURF_DEV)
    return (current, spectrum)
```

```python
import functools
import math

import jax
import jax.numpy as jnp
import numpy as np
from jax import lax
from jax.experimental import pallas as pl
from jax.experimental.pallas import tpu as pltpu
from jax.sharding import PartitionSpec as P

F32 = jnp.float32
MESH = pl.DeviceIdType.MESH
NV = 5
FREQ = 32
STEPS = 3
SURF_DEV = 128
TIME_STEP = 0.3
VISCOSITY = 0.05
PAD = 8
STAGES = ((0.0, 1.0), (0.75, 0.25), (1.0 / 3.0, 2.0 / 3.0))
AXES = ("gx", "gz", "row")


def split_dot(left, right):
    total = None
    for _ in range(3):
        part = left.astype(jnp.bfloat16)
        left = left - part.astype(F32)
        piece = jnp.dot(part, right, preferred_element_type=F32)
        total = piece if total is None else total + piece
    return total


def stencil_kernel(
    sizes, jac, cells, flow, field, samples,
    U, xr, zs, zr, rs, rr, load_sem, send_sem, recv_sem,
):
    nx, nz, nr, cx, cz, cr = sizes
    slots = cells.shape[1]
    index = [lax.axis_index(a) for a in AXES]
    counts = (nx, nz, nr)

    there = []
    for axis in range(3):
        there.append((index[axis] > 0, index[axis] < counts[axis] - 1))

    def peer(axis, side):
        ids = list(index)
        ids[axis] = index[axis] + (1 if side else -1)
        return tuple(ids)

    load = pltpu.make_async_copy(flow, U.at[0, :, :, pl.ds(PAD, cz), :], load_sem.at[0])
    load.start()

    barrier = pltpu.get_barrier_semaphore()
    for axis in range(3):
        for side in range(2):
            @pl.when(there[axis][side])
            def _():
                pl.semaphore_signal(barrier, inc=1, device_id=peer(axis, side), device_id_type=MESH)
    peers = sum(flag.astype(jnp.int32) for pair in there for flag in pair)
    pl.semaphore_wait(barrier, peers)

    for slot in range(3):
        for axis, buffer in enumerate((xr, zr, rr)):
            for side in range(2):
                @pl.when(jnp.logical_not(there[axis][side]))
                def _():
                    view = buffer.at[slot, side]
                    view[...] = jnp.zeros(view.shape, F32)
    load.wait()

    lane = lax.broadcasted_iota(jnp.int32, (cz, cr), 1)

    def copy(axis, side, slot):
        if axis == 0:
            src = U.at[slot, :, (cx - 1) if side else 0, pl.ds(PAD, cz), :]
            dst = xr.at[slot, 1 - side]
        elif axis == 1:
            src = zs.at[slot, side]
            dst = zr.at[slot, 1 - side]
        else:
            src = rs.at[slot]
            dst = rr.at[slot, 1 - side]
        return pltpu.make_async_remote_copy(
            src_ref=src, dst_ref=dst,
            send_sem=send_sem.at[axis, side, slot],
            recv_sem=recv_sem.at[axis, 1 - side, slot],
            device_id=peer(axis, side), device_id_type=MESH,
        )

    def incoming(axis, side, slot):
        if axis == 0:
            src = U.at[slot, :, 0, pl.ds(PAD, cz), :]
            dst = xr.at[slot, side]
        elif axis == 1:
            src = zs.at[slot, side]
            dst = zr.at[slot, side]
        else:
            src = rs.at[slot]
            dst = rr.at[slot, side]
        return pltpu.make_async_remote_copy(
            src_ref=src, dst_ref=dst,
            send_sem=send_sem.at[axis, side, slot],
            recv_sem=recv_sem.at[axis, side, slot],
            device_id=peer(axis, side), device_id_type=MESH,
        )

    def for_sides(axis, act):
        for side in range(2):
            @pl.when(there[axis][side])
            def _():
                act(axis, side)

    def start_x(slot):
        for_sides(0, lambda axis, side: copy(axis, side, slot).start())

    def start_zr(slot):
        packed = jnp.zeros((cz, cr), F32)
        for v in range(NV):
            for x in range(cx):
                k = 2 * (v * cx + x)
                value = U[slot, v, x, PAD:PAD + cz, :]
                zs[slot, 0, v, x:x + 1, :] = value[:1]
                zs[slot, 1, v, x:x + 1, :] = value[cz - 1:]
                turned = pltpu.roll(value, k, 1) if k else value
                packed = jnp.where((lane == k) | (lane == (k - 1) % cr), turned, packed)
        rs[slot] = packed
        for axis in (1, 2):
            for_sides(axis, lambda axis, side: copy(axis, side, slot).start())

    def wait_sent(slot):
        for axis in range(3):
            for_sides(axis, lambda axis, side: copy(axis, side, slot).wait_send())

    def wait_received(slot):
        for axis in range(3):
            for_sides(axis, lambda axis, side: incoming(axis, side, slot).wait_recv())

    def stage(j, send):
        src, dst = j, (j + 1) % 3
        keep, gain = STAGES[j]
        wait_received(src)
        for v in range(NV):
            for x in range(cx):
                U[src, v, x, PAD - 1:PAD, :] = zr[src, 0, v, x:x + 1, :]
                U[src, v, x, PAD + cz:PAD + cz + 1, :] = zr[src, 1, v, x:x + 1, :]
        halo = jnp.where(lane % 2 == 1, rr[src, 0], rr[src, 1])

        def layer(x):
            sums = [None] * NV
            rest = []
            for w in range(NV):
                center = U[src, w, x, PAD:PAD + cz, :]
                below = xr[src, 0, w] if x == 0 else U[src, w, x - 1, PAD:PAD + cz, :]
                above = xr[src, 1, w] if x == cx - 1 else U[src, w, x + 1, PAD:PAD + cz, :]
                before = U[src, w, x, PAD - 1:PAD + cz - 1, :]
                after = U[src, w, x, PAD + 1:PAD + cz + 1, :]
                k = 2 * (w * cx + x)
                turned = pltpu.roll(halo, cr - k, 1) if k else halo
                inner = pltpu.roll(jnp.where(lane == cr - 1, turned, center), 1, 1)
                outer = pltpu.roll(jnp.where(lane == 0, turned, center), cr - 1, 1)
                slopes = (above - below, after - before, outer - inner)
                beside = above + below + after + before + outer + inner
                rest.append(
                    beside * (gain * TIME_STEP * VISCOSITY)
                    + center * (gain * (1.0 - 6.0 * VISCOSITY * TIME_STEP))
                )
                for v in range(NV):
                    for d in range(3):
                        piece = slopes[d] * jac[(d * NV + v) * NV + w]
                        sums[v] = piece if sums[v] is None else sums[v] + piece
            for v in range(NV):
                value = sums[v] * (0.5 * gain * TIME_STEP) + rest[v]
                if keep:
                    value = value + U[0, v, x, PAD:PAD + cz, :] * keep
                U[dst, v, x, PAD:PAD + cz, :] = value

        layer(0)
        layer(cx - 1)
        if send is True:
            start_x(dst)
        else:
            pl.when(send)(lambda: start_x(dst))
        for x in range(1, cx - 1):
            layer(x)
        wait_sent(src)
        if send is True:
            start_zr(dst)
        else:
            pl.when(send)(lambda: start_zr(dst))

    spot = cells[...]
    spot_lane = spot % cr
    spot_row = spot // cr
    height = lax.broadcasted_iota(jnp.int32, (cr, slots), 0)
    rows = lax.broadcasted_iota(jnp.int32, (cx * cz, slots), 0)

    def sample(step):
        chosen_lane = jnp.where(height == spot_lane, 1.0, 0.0).astype(jnp.bfloat16)
        for j in range(4):
            tile = jnp.concatenate([U[0, j, x, PAD:PAD + cz, :] for x in range(cx)], axis=0)
            if j == 0:
                tile = tile + jnp.concatenate([U[0, 4, x, PAD:PAD + cz, :] for x in range(cx)], axis=0)
            picked = split_dot(tile, chosen_lane)
            picked = jnp.where(rows == spot_row, picked, 0.0)
            samples[pl.ds(step, 1), j:j + 1, :] = jnp.sum(picked, axis=0, keepdims=True)[None]

    start_x(0)
    start_zr(0)

    def step_body(step, carry):
        stage(0, True)
        stage(1, True)
        stage(2, step < STEPS - 1)
        sample(step)
        return carry

    lax.fori_loop(0, STEPS, step_body, 0)
    out = pltpu.make_async_copy(U.at[0, :, :, pl.ds(PAD, cz), :], field, load_sem.at[1])
    out.start()
    out.wait()


def run_stencil(sizes, jac, cells, flow):
    cx, cz, cr = sizes[3:]
    slots = cells.shape[1]
    return pl.pallas_call(
        functools.partial(stencil_kernel, sizes),
        out_shape=(
            jax.ShapeDtypeStruct(flow.shape, F32),
            jax.ShapeDtypeStruct((STEPS, 8, slots), F32),
        ),
        in_specs=[
            pl.BlockSpec(memory_space=pltpu.SMEM),
            pl.BlockSpec(memory_space=pltpu.VMEM),
            pl.BlockSpec(memory_space=pl.ANY),
        ],
        out_specs=(
            pl.BlockSpec(memory_space=pl.ANY),
            pl.BlockSpec(memory_space=pltpu.VMEM),
        ),
        scratch_shapes=[
            pltpu.VMEM((3, NV, cx, cz + 2 * PAD, cr), F32),
            pltpu.VMEM((3, 2, NV, cz, cr), F32),
            pltpu.VMEM((3, 2, NV, cx, cr), F32),
            pltpu.VMEM((3, 2, NV, cx, cr), F32),
            pltpu.VMEM((3, cz, cr), F32),
            pltpu.VMEM((3, 2, cz, cr), F32),
            pltpu.SemaphoreType.DMA((2,)),
            pltpu.SemaphoreType.DMA((3, 2, 3)),
            pltpu.SemaphoreType.DMA((3, 2, 3)),
        ],
        compiler_params=pltpu.CompilerParams(
            collective_id=0, has_side_effects=True, vmem_limit_bytes=40 << 20
        ),
        name="stencil",
    )(jac, cells, flow)


def poly(x, coefficients):
    total = jnp.full_like(x, coefficients[-1])
    for c in coefficients[-2::-1]:
        total = total * x + c
    return total


SIN = [(-1.0) ** n / math.factorial(2 * n + 1) for n in range(9)]
COS = [(-1.0) ** n / math.factorial(2 * n) for n in range(10)]


def radiate_kernel(sizes, table, cells, blocks, watch, history, samples, out, held, spec, place, seat, sem):
    nx, nz, nr, cx, cz, cr = sizes
    slots = cells.shape[1]
    times = history.shape[2]
    grid = (nx * cx, nz * cz, nr * cr)
    groups = slots // 128
    observers = watch.shape[0]
    copies = [
        pltpu.make_async_copy(history.at[:, v, :], held.at[v], sem.at[v]) for v in range(NV)
    ]
    for c in copies:
        c.start()
    spot = cells[...]
    index = [lax.axis_index(a) for a in AXES]
    place[0:1, :] = (index[0] * cx + spot // (cz * cr)).astype(F32) + 0.5
    place[1:2, :] = (index[1] * cz + spot // cr % cz).astype(F32) + 0.5
    place[2:3, :] = (index[2] * cr + spot % cr).astype(F32) + 0.5
    for c in copies:
        c.wait()
    fourier = table[...]
    time = lax.broadcasted_iota(jnp.int32, fourier.shape, 1)
    early = jnp.where(time < times - STEPS, fourier, 0.0)
    for j in range(4):
        signal = held[j] + held[4] if j == 0 else held[j]
        spectrum = lax.dot_general(
            early, signal, (((1,), (1,)), ((), ())),
            precision=lax.Precision.HIGHEST, preferred_element_type=F32,
        )
        for t in range(STEPS):
            column = fourier[:, times - STEPS + t:times - STEPS + t + 1]
            spectrum = spectrum + column * samples[t, j:j + 1, :]
        spec[j] = spectrum
    live = lax.broadcasted_iota(jnp.int32, (8, 128), 1)
    live_count = blocks[0] * 64
    unit = 2.0 / grid[2]
    middle = 2.3
    lane = lax.broadcasted_iota(jnp.int32, (8, 128), 1)
    norm = 1.0 / math.sqrt(nx * nz * nr * SURF_DEV)

    def tile(i, carry):
        rows = pl.ds(pl.multiple_of(i * 8, 8), 8)
        seats = watch[rows, :]
        at = (
            seats[:, 0:1] * float(grid[0]),
            seats[:, 1:2] * float(grid[1]),
            (1.25 + 0.75 * seats[:, 2:3]) * float(grid[2]),
        )
        state = []
        for g in range(groups):
            cols = slice(g * 128, (g + 1) * 128)
            away = [at[d] - place[d:d + 1, cols] for d in range(3)]
            square = away[0] * away[0] + away[1] * away[1] + away[2] * away[2]
            distance = jnp.sqrt(square)
            inverse = 1.0 / distance
            unit_vec = [w * inverse for w in away]
            angle = distance * unit - middle
            sq = angle * angle
            sine = angle * poly(sq, SIN)
            cosine = poly(sq, COS)
            cm, sm = math.cos(middle), math.sin(middle)
            zr = cosine * cm - sine * sm
            zi = -(sine * cm + cosine * sm)
            amp = jnp.where(live + g * 128 < live_count, inverse * (grid[2] * norm), 0.0)
            near = inverse * (1.0 / unit)
            state.append([unit_vec, near, zr, zi, amp * zr, amp * zi])
        result = jnp.zeros((8, 128), F32)
        for f in range(FREQ):
            real, imag = None, None
            for g in range(groups):
                cols = slice(g * 128, (g + 1) * 128)
                unit_vec, near, zr, zi, ur, ui = state[g]
                sr = [spec[j, f:f + 1, cols] for j in range(4)]
                si = [spec[j, FREQ + f:FREQ + f + 1, cols] for j in range(4)]
                dr = unit_vec[0] * sr[1] + unit_vec[1] * sr[2] + unit_vec[2] * sr[3]
                di = unit_vec[0] * si[1] + unit_vec[1] * si[2] + unit_vec[2] * si[3]
                w = near * (1.0 / (f + 1))
                gr = w * dr - (si[0] + di)
                gi = w * di + (sr[0] + dr)
                pr = ur * gr - ui * gi
                pi = ur * gi + ui * gr
                real = pr if real is None else real + pr
                imag = pi if imag is None else imag + pi
                if f < FREQ - 1:
                    state[g][4] = ur * zr - ui * zi
                    state[g][5] = ur * zi + ui * zr
            result = jnp.where(lane == f, jnp.sum(real, axis=1, keepdims=True), result)
            result = jnp.where(lane == FREQ + f, jnp.sum(imag, axis=1, keepdims=True), result)
        out[rows, :] = result
        return carry

    lax.fori_loop(0, observers // 8, tile, 0)


def run_radiate(sizes, table, cells, blocks, watch, history, samples):
    slots = cells.shape[1]
    vm = pl.BlockSpec(memory_space=pltpu.VMEM)
    return pl.pallas_call(
        functools.partial(radiate_kernel, sizes),
        out_shape=jax.ShapeDtypeStruct((watch.shape[0], 128), F32),
        in_specs=[vm, vm, pl.BlockSpec(memory_space=pltpu.SMEM), vm, pl.BlockSpec(memory_space=pl.ANY), vm],
        out_specs=vm,
        scratch_shapes=[
            pltpu.VMEM((NV, slots, history.shape[2]), F32),
            pltpu.VMEM((4, 2 * FREQ, slots), F32),
            pltpu.VMEM((8, slots), F32),
            pltpu.VMEM((8, 128), F32),
            pltpu.SemaphoreType.DMA((NV,)),
        ],
        compiler_params=pltpu.CompilerParams(vmem_limit_bytes=40 << 20),
        name="radiate",
    )(table, cells, blocks, watch, history, samples)


def reduce_kernel(counts, value, out, got, rows, last, send1, recv1, send2, recv2):
    nx, nz, nr = counts
    plane = nz * nr
    a, b, c = [lax.axis_index(x) for x in AXES]
    place = b * nr + c

    def along(d):
        return (lax.rem(a + d, nx), b, c)

    def across(d):
        other = lax.rem(place + d, plane)
        return (a, other // nr, lax.rem(other, nr))

    barrier = pltpu.get_barrier_semaphore()
    for d in range(1, nx):
        pl.semaphore_signal(barrier, inc=1, device_id=along(d), device_id_type=MESH)
    for d in range(1, plane):
        pl.semaphore_signal(barrier, inc=1, device_id=across(d), device_id_type=MESH)
    pl.semaphore_wait(barrier, nx - 1 + plane - 1)

    first = []
    for d in range(1, nx):
        to = lax.rem(a + d, nx)
        first.append(pltpu.make_async_remote_copy(
            src_ref=value.at[pl.ds(pl.multiple_of(to * plane, plane), plane)],
            dst_ref=got.at[d - 1], send_sem=send1.at[d - 1], recv_sem=recv1.at[d - 1],
            device_id=along(d), device_id_type=MESH,
        ))
    for x in first:
        x.start()
    total = value[pl.ds(pl.multiple_of(a * plane, plane), plane)]
    for d in range(1, nx):
        first[d - 1].wait_recv()
        total = total + got[d - 1]
    rows[...] = total[:, None, :]
    second = []
    for d in range(1, plane):
        to = lax.rem(place + d, plane)
        second.append(pltpu.make_async_remote_copy(
            src_ref=rows.at[to], dst_ref=last.at[d - 1],
            send_sem=send2.at[d - 1], recv_sem=recv2.at[d - 1],
            device_id=across(d), device_id_type=MESH,
        ))
    for x in second:
        x.start()
    for x in second:
        x.wait_recv()
    total = rows[place] + jnp.sum(last[...], axis=0)
    out[...] = total[:, :out.shape[1]]
    for x in first + second:
        x.wait_send()


def run_reduce(counts, value):
    nx, nz, nr = counts
    plane = nz * nr
    return pl.pallas_call(
        functools.partial(reduce_kernel, counts),
        out_shape=jax.ShapeDtypeStruct((1, 2 * FREQ), F32),
        in_specs=[pl.BlockSpec(memory_space=pltpu.VMEM)],
        out_specs=pl.BlockSpec(memory_space=pltpu.VMEM),
        scratch_shapes=[
            pltpu.VMEM((nx - 1, plane, 128), F32),
            pltpu.VMEM((plane, 1, 128), F32),
            pltpu.VMEM((plane - 1, 1, 128), F32),
            pltpu.SemaphoreType.DMA((nx - 1,)),
            pltpu.SemaphoreType.DMA((nx - 1,)),
            pltpu.SemaphoreType.DMA((plane - 1,)),
            pltpu.SemaphoreType.DMA((plane - 1,)),
        ],
        compiler_params=pltpu.CompilerParams(
            collective_id=1, has_side_effects=True, vmem_limit_bytes=40 << 20
        ),
        name="reduce",
    )(value)


def fourier_table(samples):
    turns = np.arange(1, FREQ + 1)[:, None] * np.arange(samples)[None, :] % samples
    angles = 2.0 * np.pi * turns / samples
    return (np.concatenate([np.cos(angles), -np.sin(angles)]) / np.sqrt(samples)).astype(np.float32)


def solution(mesh):
    counts = tuple(mesh.shape[a] for a in AXES)

    def per_device(flow, jacobian, history, cell, blocks, observers):
        sizes = counts + flow.shape[1:]
        cells = cell.reshape(1, -1)
        field, samples = run_stencil(sizes, jacobian.reshape(-1), cells, flow)
        table = jnp.asarray(fourier_table(history.shape[2]))
        value = run_radiate(sizes, table, cells, blocks.reshape(-1), observers.T, history, samples)
        return field, run_reduce(counts, value)

    return jax.shard_map(
        per_device,
        mesh=mesh,
        in_specs=(
            P(None, "gx", "gz", "row"),
            P(),
            P(AXES, None, None),
            P(AXES, None),
            P("row", ("gx", "gz")),
            P(),
        ),
        out_specs=(P(None, "gx", "gz", "row"), P(AXES, None)),
        check_vma=False,
    )
```

```python
import functools
import math

import jax
import jax.numpy as jnp
import numpy as np
from jax import lax
from jax.experimental import pallas as pl
from jax.experimental.pallas import tpu as pltpu
from jax.sharding import PartitionSpec as P

F32 = jnp.float32
MESH = pl.DeviceIdType.MESH
NV = 5
FREQ = 32
STEPS = 3
SURF_DEV = 128
TIME_STEP = 0.3
VISCOSITY = 0.05
PAD = 8
KEEP = (0.0, 0.75, 1.0 / 3.0)
GAIN = (1.0, 0.25, 2.0 / 3.0)
AXES = ("gx", "gz", "row")
OLD = (0, 5, 5, 5, 4, 4, 3, 3, 3)
NEW = ((0, 0, 0, 2, 4, 4, 0, 0, 0), (0, 0, 0, 0, 0, 0, 7, 8, 8))


def split_dot(left, right):
    total = None
    for _ in range(3):
        part = left.astype(jnp.bfloat16)
        left = left - part.astype(F32)
        piece = jnp.dot(part, right, preferred_element_type=F32)
        total = piece if total is None else total + piece
    return total


def poly(x, coefficients):
    total = jnp.full_like(x, coefficients[-1])
    for c in coefficients[-2::-1]:
        total = total * x + c
    return total


SIN = [(-1.0) ** n / math.factorial(2 * n + 1) for n in range(9)]
COS = [(-1.0) ** n / math.factorial(2 * n) for n in range(10)]


def fourier_table(samples):
    turns = np.arange(1, FREQ + 1)[:, None] * np.arange(samples)[None, :] % samples
    angles = 2.0 * np.pi * turns / samples
    return (np.concatenate([np.cos(angles), -np.sin(angles)]) / np.sqrt(samples)).astype(np.float32)


def turn_rows(samples):
    f = np.arange(1, FREQ + 1)
    zero = np.zeros(FREQ)

    def turned(factor, both):
        re, im = factor.real, factor.imag
        return [
            np.concatenate([re, re, re, re] if both else [re, re, zero, zero]),
            np.concatenate([-im, zero, -im, zero] if both else [-im, zero, zero, zero]),
            np.concatenate([zero, im, zero, im] if both else [zero, im, zero, zero]),
        ]

    last = samples - 1
    rows = turned(-1j * np.exp(2j * np.pi * f * last / samples), False)
    for t in range(STEPS - 1):
        rows += turned(np.exp(2j * np.pi * f * (STEPS - 1 - t) / samples), True)
    w = np.exp(-2j * np.pi * f * last / samples)
    rows += [
        np.concatenate([-w.imag, -w.imag, zero, zero]),
        np.concatenate([-w.real, w.imag / f, zero, zero]),
        np.concatenate([w.real / f, w.real / f, zero, zero]),
        np.concatenate([-w.imag / f, w.real, zero, zero]),
    ]
    rows += [np.zeros(128)] * (-len(rows) % 8)
    return np.stack(rows).astype(np.float32)


def whole_kernel(
    sizes, flow, cells_in, watch_in, blocks_in, jac_in, table_in, turns_in, history, field, out,
    U, cells, watch, blocks, jac, table, turns, held,
    xr, zs, zr, rs, rr, spec, samples, geo, tab, seats, line, value, got, rows, last,
    load_sem, send_sem, recv_sem, send1, recv1, send2, recv2,
):
    nx, nz, nr, cx, cz, cr = sizes
    grid = (nx * cx, nz * cz, nr * cr)
    plane = nz * nr
    slots = line.shape[1]
    groups = slots // 128
    times = held.shape[2]
    observers = watch.shape[1]
    tiles = observers // 8
    stages = 3 * STEPS
    index = [lax.axis_index(a) for a in AXES]
    counts = (nx, nz, nr)
    a, b, c = index
    seat = b * nr + c

    loads = [
        pltpu.make_async_copy(source, target, load_sem.at[n])
        for n, (source, target) in enumerate((
            (flow, U.at[0, :, :, pl.ds(PAD, cz), :]),
            (cells_in, cells), (watch_in, watch), (blocks_in, blocks),
            (jac_in, jac), (table_in, table), (turns_in, turns), (history, held),
        ))
    ]
    for x in loads:
        x.start()

    def along(d):
        return (lax.rem(a + d, nx), b, c)

    def across(d):
        other = lax.rem(seat + d, plane)
        return (a, other // nr, lax.rem(other, nr))

    barrier = pltpu.get_barrier_semaphore()
    for d in range(1, nx):
        pl.semaphore_signal(barrier, inc=1, device_id=along(d), device_id_type=MESH)
    for d in range(1, plane):
        pl.semaphore_signal(barrier, inc=1, device_id=across(d), device_id_type=MESH)

    there = [(index[axis] > 0, index[axis] < counts[axis] - 1) for axis in range(3)]

    def peer(axis, side):
        ids = list(index)
        ids[axis] = index[axis] + (1 if side else -1)
        return tuple(ids)

    for slot in range(3):
        for axis, buffer in enumerate((xr, zr, rr)):
            for side in range(2):
                @pl.when(jnp.logical_not(there[axis][side]))
                def _():
                    view = buffer.at[slot, side]
                    view[...] = jnp.zeros(view.shape, F32)

    for x in loads[1:3]:
        x.wait()
    for i in range(cells.shape[0]):
        line[0:1, 64 * i:64 * i + 64] = cells[i:i + 1, :]
    for d in range(3):
        for g in range(observers // 128):
            wide = jnp.broadcast_to(watch[d:d + 1, g * 128:g * 128 + 128], (128, 128))
            columns = wide.T
            for n in range(128 // plane):
                seats[d, pl.ds(g * (128 // plane) + n, plane, stride=nx), :] = columns[n * plane:(n + 1) * plane]

    lane = lax.broadcasted_iota(jnp.int32, (cz, cr), 1)
    lane8 = lax.broadcasted_iota(jnp.int32, (8, 128), 1)

    unit = 2.0 / grid[2]
    middle = 2.3
    norm = 1.0 / math.sqrt(nx * nz * nr * SURF_DEV)

    def geometry(i, carry):
        limit = blocks[0, 0] * 64
        span = pl.ds(pl.multiple_of(i * 32, 32), 32)
        at = (
            seats[0, span, :] * float(grid[0]),
            seats[1, span, :] * float(grid[1]),
            (1.25 + 0.75 * seats[2, span, :]) * float(grid[2]),
        )
        for g in range(groups):
            cols = slice(g * 128, (g + 1) * 128)
            spot = line[0:1, cols]
            place = (
                (index[0] * cx + spot // (cz * cr)).astype(F32) + 0.5,
                (index[1] * cz + spot // cr % cz).astype(F32) + 0.5,
                (index[2] * cr + spot % cr).astype(F32) + 0.5,
            )
            away = [at[d] - place[d] for d in range(3)]
            square = away[0] * away[0] + away[1] * away[1] + away[2] * away[2]
            distance = jnp.sqrt(square)
            inverse = 1.0 / distance
            for d in range(3):
                geo[d, span, cols] = away[d] * inverse
            geo[3, span, cols] = inverse * (1.0 / unit)
            angle = distance * unit - middle
            sq = angle * angle
            sine = angle * poly(sq, SIN)
            cosine = poly(sq, COS)
            cm, sm = math.cos(middle), math.sin(middle)
            step_r = cosine * cm - sine * sm
            step_i = -(sine * cm + cosine * sm)
            amp = jnp.where(lane + g * 128 < limit, inverse * (grid[2] * norm), 0.0)
            geo[4, span, cols] = step_r
            geo[5, span, cols] = step_i
            geo[6, span, cols] = amp * step_r
            geo[7, span, cols] = amp * step_i
        return carry

    def spectra():
        fourier = table[...]
        time = lax.broadcasted_iota(jnp.int32, fourier.shape, 1)
        early = jnp.where(time < times - STEPS, fourier, 0.0)
        for j in range(4):
            signal = held[j] + held[4] if j == 0 else held[j]
            spec[j] = lax.dot_general(
                early, signal, (((1,), (1,)), ((), ())),
                precision=lax.Precision.HIGHEST, preferred_element_type=F32,
            )

    def grow(step):
        at = times - STEPS + step
        for j in range(4):
            spec[j] = spec[j] + table[:, at:at + 1] * samples[step, j:j + 1, :]

    def turned(what, first):
        return (
            what * turns[first:first + 1, :]
            + pltpu.roll(what, 96, 1) * turns[first + 1:first + 2, :]
            + pltpu.roll(what, 32, 1) * turns[first + 2:first + 3, :]
        )

    def old_tile(i, carry):
        span = pl.ds(pl.multiple_of(i * 8, 8), 8)
        state = []
        for g in range(groups):
            state.append([geo[k, span, g * 128:(g + 1) * 128] for k in range(8)])
        result = jnp.zeros((8, 128), F32)
        for f in range(FREQ):
            real, imag = None, None
            for g in range(groups):
                cols = slice(g * 128, (g + 1) * 128)
                ex, ey, ez, near, zre, zim, ur, ui = state[g]
                tab[i, f, 0, :, cols] = ur
                tab[i, f, 1, :, cols] = ui
                sr = [spec[j, f:f + 1, cols] for j in range(4)]
                si = [spec[j, FREQ + f:FREQ + f + 1, cols] for j in range(4)]
                dr = ex * sr[1] + ey * sr[2] + ez * sr[3]
                di = ex * si[1] + ey * si[2] + ez * si[3]
                w = near * (1.0 / (f + 1))
                gr = w * dr - (si[0] + di)
                gi = w * di + (sr[0] + dr)
                pr = ur * gr - ui * gi
                pi = ur * gi + ui * gr
                real = pr if real is None else real + pr
                imag = pi if imag is None else imag + pi
                if f < FREQ - 1:
                    state[g][6] = ur * zre - ui * zim
                    state[g][7] = ur * zim + ui * zre
            result = jnp.where(lane8 == f, jnp.sum(real, axis=1, keepdims=True), result)
            result = jnp.where(lane8 == FREQ + f, jnp.sum(imag, axis=1, keepdims=True), result)
        value[span, :] = turned(result, 0)
        return carry

    def new_tile(i, t):
        span = pl.ds(pl.multiple_of(i * 8, 8), 8)
        weights = []
        for g in range(groups):
            cols = slice(g * 128, (g + 1) * 128)
            own = [samples[t, j:j + 1, cols] * (1.0 / math.sqrt(times)) for j in range(4)]
            dip = sum(geo[d, span, cols] * own[d + 1] for d in range(3))
            weights.append((own[0] + dip, geo[3, span, cols] * dip))
        what = jnp.zeros((8, 128), F32)
        for f in range(FREQ):
            phases = [[tab[i, f, n, :, g * 128:(g + 1) * 128] for n in range(2)] for g in range(groups)]
            for k in range(4):
                total = sum(weights[g][k // 2] * phases[g][k % 2] for g in range(groups))
                total = jnp.sum(total, axis=1, keepdims=True)
                what = jnp.where(lane8 == FREQ * k + f, total, what)
        return span, what

    def middle_tile(t, i, carry):
        span, what = new_tile(i, t)
        value[span, :] = value[span, :] + turned(what, 3 * (t + 1))
        return carry

    def last_tile(i, carry):
        span, what = new_tile(i, STEPS - 1)
        value[span, :] = value[span, :] + what
        return carry

    def fill(k):
        def upto(counts, i):
            return sum(jnp.where(i > n, count, 0) for n, count in enumerate(counts))

        for counts, act in (
            (OLD, old_tile), (NEW[0], functools.partial(middle_tile, 0)), (NEW[1], functools.partial(middle_tile, 1)),
        ):
            lax.fori_loop(upto(counts, k), upto(counts, k + 1), act, 0)

    def copy(axis, side, slot, mine):
        land = 1 - side if mine else side
        if axis == 0:
            src = U.at[slot, :, (cx - 1) if side else 0, pl.ds(PAD, cz), :]
            dst = xr.at[slot, land]
        elif axis == 1:
            src = zs.at[slot, side]
            dst = zr.at[slot, land]
        else:
            src = rs.at[slot]
            dst = rr.at[slot, land]
        return pltpu.make_async_remote_copy(
            src_ref=src, dst_ref=dst,
            send_sem=send_sem.at[axis, side, slot],
            recv_sem=recv_sem.at[axis, land, slot],
            device_id=peer(axis, side), device_id_type=MESH,
        )

    def for_sides(axis, act):
        for side in range(2):
            @pl.when(there[axis][side])
            def _():
                act(axis, side)

    def start_x(slot):
        for_sides(0, lambda axis, side: copy(axis, side, slot, True).start())

    def start_zr(slot):
        packed = jnp.zeros((cz, cr), F32)
        for v in range(NV):
            for x in range(cx):
                k = 2 * (v * cx + x)
                what = U[slot, v, x, PAD:PAD + cz, :]
                zs[slot, 0, v, x:x + 1, :] = what[:1]
                zs[slot, 1, v, x:x + 1, :] = what[cz - 1:]
                moved = pltpu.roll(what, k, 1) if k else what
                packed = jnp.where((lane == k) | (lane == (k - 1) % cr), moved, packed)
        rs[slot] = packed
        for axis in (2, 1):
            for_sides(axis, lambda axis, side: copy(axis, side, slot, True).start())

    def wait_received(slot):
        for axis in (1, 2, 0):
            for_sides(axis, lambda axis, side: copy(axis, side, slot, False).wait_recv())

    def wait_sent(slot):
        for axis in range(3):
            for_sides(axis, lambda axis, side: copy(axis, side, slot, True).wait_send())

    def pick(j, choices):
        return jnp.where(j == 0, choices[0], jnp.where(j == 1, choices[1], choices[2])).astype(F32)

    def stage(k):
        src, dst = lax.rem(k, 3), lax.rem(k + 1, 3)
        keep, gain = pick(src, KEEP), pick(src, GAIN)
        by_slope = gain * (0.5 * TIME_STEP)
        by_side = gain * (TIME_STEP * VISCOSITY)
        by_center = gain * (1.0 - 6.0 * VISCOSITY * TIME_STEP)
        for v in range(NV):
            for x in range(cx):
                U[src, v, x, PAD - 1:PAD, :] = zr[src, 0, v, x:x + 1, :]
                U[src, v, x, PAD + cz:PAD + cz + 1, :] = zr[src, 1, v, x:x + 1, :]
        halo = jnp.where(lane % 2 == 1, rr[src, 0], rr[src, 1])

        def layer(x):
            sums = [None] * NV
            rest = []
            for w in range(NV):
                center = U[src, w, x, PAD:PAD + cz, :]
                below = xr[src, 0, w] if x == 0 else U[src, w, x - 1, PAD:PAD + cz, :]
                above = xr[src, 1, w] if x == cx - 1 else U[src, w, x + 1, PAD:PAD + cz, :]
                before = U[src, w, x, PAD - 1:PAD + cz - 1, :]
                after = U[src, w, x, PAD + 1:PAD + cz + 1, :]
                n = 2 * (w * cx + x)
                moved = pltpu.roll(halo, cr - n, 1) if n else halo
                inner = pltpu.roll(jnp.where(lane == cr - 1, moved, center), 1, 1)
                outer = pltpu.roll(jnp.where(lane == 0, moved, center), cr - 1, 1)
                slopes = (above - below, after - before, outer - inner)
                beside = above + below + after + before + outer + inner
                rest.append(beside * by_side + center * by_center)
                for v in range(NV):
                    for d in range(3):
                        piece = slopes[d] * jac[v, d, w]
                        sums[v] = piece if sums[v] is None else sums[v] + piece
            for v in range(NV):
                what = sums[v] * by_slope + rest[v] + U[0, v, x, PAD:PAD + cz, :] * keep
                U[dst, v, x, PAD:PAD + cz, :] = what

        layer(0)
        layer(cx - 1)
        pl.when(k < stages - 1)(lambda: start_x(dst))
        for x in range(1, cx - 1):
            layer(x)

    height = lax.broadcasted_iota(jnp.int32, (cr, slots), 0)
    rows_of = lax.broadcasted_iota(jnp.int32, (cx * cz, slots), 0)

    def sample(step):
        spot = line[...]
        chosen_lane = jnp.where(height == spot % cr, 1.0, 0.0).astype(jnp.bfloat16)
        for j in range(4):
            tile = jnp.concatenate([U[0, j, x, PAD:PAD + cz, :] for x in range(cx)], axis=0)
            if j == 0:
                tile = tile + jnp.concatenate([U[0, 4, x, PAD:PAD + cz, :] for x in range(cx)], axis=0)
            picked = split_dot(tile, chosen_lane)
            picked = jnp.where(rows_of == spot // cr, picked, 0.0)
            picked = jnp.sum(picked, axis=0, keepdims=True)
            samples[step, j:j + 1, :] = picked

    loads[0].wait()
    pl.semaphore_wait(barrier, nx - 1 + plane - 1)
    start_x(0)

    def body(k, carry):
        slot = lax.rem(k, 3)
        start_zr(slot)

        @pl.when(k == 0)
        def _():
            for x in loads[3:]:
                x.wait()
            lax.fori_loop(0, observers // 32, geometry, 0)
            spectra()

        for step in range(STEPS - 1):
            @pl.when(k == 3 * step + 3)
            def _():
                sample(step)
                grow(step)

        fill(k)
        wait_received(slot)
        stage(k)
        wait_sent(slot)
        return carry

    lax.fori_loop(0, stages, body, 0)
    result = pltpu.make_async_copy(U.at[0, :, :, pl.ds(PAD, cz), :], field, load_sem.at[0])
    result.start()
    sample(STEPS - 1)

    def first(d):
        to = lax.rem(seat + d, plane)
        return pltpu.make_async_remote_copy(
            src_ref=value.at[pl.ds(pl.multiple_of(to * nx, nx), nx)],
            dst_ref=got.at[d - 1], send_sem=send1.at[d - 1], recv_sem=recv1.at[d - 1],
            device_id=across(d), device_id_type=MESH,
        )

    def second(d):
        to = lax.rem(a + d, nx)
        return pltpu.make_async_remote_copy(
            src_ref=rows.at[to], dst_ref=last.at[d - 1],
            send_sem=send2.at[d - 1], recv_sem=recv2.at[d - 1],
            device_id=along(d), device_id_type=MESH,
        )

    def chunk(d, carry):
        last_tile(lax.rem(seat + d, plane), 0)
        first(d).start()
        return carry

    lax.fori_loop(1, plane, chunk, 0)
    last_tile(seat, 0)
    total = value[pl.ds(pl.multiple_of(seat * nx, nx), nx)]
    for d in range(1, plane):
        first(d).wait_recv()
        total = total + got[d - 1]
    rows[...] = total[:, None, :]
    for d in range(1, nx):
        second(d).start()
    for d in range(1, nx):
        second(d).wait_recv()
    total = rows[a] + jnp.sum(last[...], axis=0)
    spectrum = total * turns[9:10, :]
    for n, shift in enumerate((96, 64, 32)):
        spectrum = spectrum + pltpu.roll(total, shift, 1) * turns[10 + n:11 + n, :]
    out[...] = spectrum[:, :2 * FREQ]
    for d in range(1, plane):
        first(d).wait_send()
    for d in range(1, nx):
        second(d).wait_send()
    result.wait()


def finish_kernel(field_in, spectrum_in, field, spectrum, held, line, sem):
    pairs = [(field_in.at[v], held.at[v], field.at[v]) for v in range(NV)]
    pairs.append((spectrum_in, line, spectrum))
    into = [pltpu.make_async_copy(p[0], p[1], sem.at[0, n]) for n, p in enumerate(pairs)]
    back = [pltpu.make_async_copy(p[1], p[2], sem.at[1, n]) for n, p in enumerate(pairs)]
    for x in into:
        x.start()
    for x, y in zip(into, back):
        x.wait()
        y.start()
    for y in back:
        y.wait()


def finish(field, spectrum):
    hbm = pl.BlockSpec(memory_space=pltpu.HBM)
    return pl.pallas_call(
        finish_kernel,
        out_shape=(
            jax.ShapeDtypeStruct(field.shape, F32),
            jax.ShapeDtypeStruct(spectrum.shape, F32),
        ),
        in_specs=[hbm, hbm],
        out_specs=(hbm, hbm),
        scratch_shapes=[
            pltpu.VMEM(field.shape, F32),
            pltpu.VMEM(spectrum.shape, F32),
            pltpu.SemaphoreType.DMA((2, NV + 1)),
        ],
        compiler_params=pltpu.CompilerParams(vmem_limit_bytes=63 << 20),
        name="finish",
    )(field, spectrum)


def solution(mesh):
    counts = tuple(mesh.shape[a] for a in AXES)
    nx, nz, nr = counts
    plane = nz * nr
    assert nx == 8

    def per_device(flow, jacobian, history, cell, blocks, observers):
        sizes = counts + flow.shape[1:]
        cx, cz, cr = flow.shape[1:]
        slots, times = history.shape[0], history.shape[2]
        seats = observers.shape[1]
        hbm = pl.BlockSpec(memory_space=pltpu.HBM)
        dma = pltpu.SemaphoreType.DMA
        lanes = turn_rows(times)
        field, spectrum = pl.pallas_call(
            functools.partial(whole_kernel, sizes),
            out_shape=(
                jax.ShapeDtypeStruct(flow.shape, F32),
                jax.ShapeDtypeStruct((1, 2 * FREQ), F32),
            ),
            in_specs=[hbm] * 8,
            out_specs=(hbm, pl.BlockSpec(memory_space=pltpu.VMEM)),
            scratch_shapes=[
                pltpu.VMEM((3, NV, cx, cz + 2 * PAD, cr), F32),
                pltpu.VMEM(cell.shape, jnp.int32),
                pltpu.VMEM(observers.shape, F32),
                pltpu.SMEM(blocks.shape, jnp.int32),
                pltpu.SMEM((NV, 3, NV), F32),
                pltpu.VMEM((2 * FREQ, times), F32),
                pltpu.VMEM(lanes.shape, F32),
                pltpu.VMEM((NV, slots, times), F32),
                pltpu.VMEM((3, 2, NV, cz, cr), F32),
                pltpu.VMEM((3, 2, NV, cx, cr), F32),
                pltpu.VMEM((3, 2, NV, cx, cr), F32),
                pltpu.VMEM((3, cz, cr), F32),
                pltpu.VMEM((3, 2, cz, cr), F32),
                pltpu.VMEM((4, 2 * FREQ, slots), F32),
                pltpu.VMEM((STEPS, 8, slots), F32),
                pltpu.VMEM((8, seats, slots), F32),
                pltpu.VMEM((seats // 8, FREQ, 2, 8, slots), F32),
                pltpu.VMEM((3, seats, 128), F32),
                pltpu.VMEM((1, slots), jnp.int32),
                pltpu.VMEM((seats, 128), F32),
                pltpu.VMEM((plane - 1, nx, 128), F32),
                pltpu.VMEM((nx, 1, 128), F32),
                pltpu.VMEM((nx - 1, 1, 128), F32),
                dma((8,)),
                dma((3, 2, 3)),
                dma((3, 2, 3)),
                dma((plane - 1,)),
                dma((plane - 1,)),
                dma((nx - 1,)),
                dma((nx - 1,)),
            ],
            compiler_params=pltpu.CompilerParams(
                collective_id=0, has_side_effects=True, vmem_limit_bytes=63 << 20
            ),
            name="whole",
        )(
            flow, cell, observers, blocks, jacobian.transpose(1, 0, 2),
            jnp.asarray(fourier_table(times)), jnp.asarray(lanes), history.transpose(1, 0, 2),
        )
        return finish(field, spectrum)

    return jax.shard_map(
        per_device,
        mesh=mesh,
        in_specs=(
            P(None, "gx", "gz", "row"),
            P(),
            P(AXES, None, None),
            P(AXES, None),
            P("row", ("gx", "gz")),
            P(),
        ),
        out_specs=(P(None, "gx", "gz", "row"), P(AXES, None)),
        check_vma=False,
    )
```

```python
import functools
import math

import jax
import jax.numpy as jnp
import numpy as np
from jax import lax
from jax.experimental import pallas as pl
from jax.experimental.pallas import tpu as pltpu
from jax.sharding import PartitionSpec as P

F32 = jnp.float32
MESH = pl.DeviceIdType.MESH
NV = 5
FREQ = 32
STEPS = 3
SURF_DEV = 128
TIME_STEP = 0.3
VISCOSITY = 0.05
PAD = 8
KEEP = (0.0, 0.75, 1.0 / 3.0)
GAIN = (1.0, 0.25, 2.0 / 3.0)
AXES = ("gx", "gz", "row")
OLD = (0, 5, 5, 4, 4, 4, 3, 3, 4)
NEW = ((0, 0, 0, 2, 4, 4, 0, 0, 0), (0, 0, 0, 0, 0, 0, 7, 8, 7))


def split_dot(left, right):
    total = None
    for _ in range(3):
        part = left.astype(jnp.bfloat16)
        left = left - part.astype(F32)
        piece = jnp.dot(part, right, preferred_element_type=F32)
        total = piece if total is None else total + piece
    return total


def poly(x, coefficients):
    total = jnp.full_like(x, coefficients[-1])
    for c in coefficients[-2::-1]:
        total = total * x + c
    return total


SIN = [(-1.0) ** n / math.factorial(2 * n + 1) for n in range(9)]
COS = [(-1.0) ** n / math.factorial(2 * n) for n in range(10)]


def fourier_table(samples):
    turns = np.arange(1, FREQ + 1)[:, None] * np.arange(samples)[None, :] % samples
    angles = 2.0 * np.pi * turns / samples
    return (np.concatenate([np.cos(angles), -np.sin(angles)]) / np.sqrt(samples)).astype(np.float32)


def turn_rows(samples):
    f = np.arange(1, FREQ + 1)
    zero = np.zeros(FREQ)

    def turned(factor, both):
        re, im = factor.real, factor.imag
        return [
            np.concatenate([re, re, re, re] if both else [re, re, zero, zero]),
            np.concatenate([-im, zero, -im, zero] if both else [-im, zero, zero, zero]),
            np.concatenate([zero, im, zero, im] if both else [zero, im, zero, zero]),
        ]

    last = samples - 1
    rows = turned(-1j * np.exp(2j * np.pi * f * last / samples), False)
    for t in range(STEPS - 1):
        rows += turned(np.exp(2j * np.pi * f * (STEPS - 1 - t) / samples), True)
    w = np.exp(-2j * np.pi * f * last / samples)
    rows += [
        np.concatenate([-w.imag, -w.imag, zero, zero]),
        np.concatenate([-w.real, w.imag / f, zero, zero]),
        np.concatenate([w.real / f, w.real / f, zero, zero]),
        np.concatenate([-w.imag / f, w.real, zero, zero]),
    ]
    rows += [np.zeros(128)] * (-len(rows) % 8)
    return np.stack(rows).astype(np.float32)


def whole_kernel(
    sizes, flow, cells_in, watch_in, blocks_in, jac_in, table_in, turns_in, history, field, out,
    U, cells, watch, blocks, jac, table, turns, held,
    xr, zs, zr, rs, rr, spec, samples, geo, tab, seats, line, value, got, rows, last,
    load_sem, send_sem, recv_sem, send1, recv1, send2, recv2,
):
    nx, nz, nr, cx, cz, cr = sizes
    grid = (nx * cx, nz * cz, nr * cr)
    plane = nz * nr
    slots = line.shape[1]
    groups = slots // 128
    times = held.shape[2]
    observers = watch.shape[1]
    tiles = observers // 8
    stages = 3 * STEPS
    index = [lax.axis_index(a) for a in AXES]
    counts = (nx, nz, nr)
    a, b, c = index
    seat = b * nr + c

    def along(d):
        return (lax.rem(a + d, nx), b, c)

    def across(d):
        other = lax.rem(seat + d, plane)
        return (a, other // nr, lax.rem(other, nr))

    barrier = pltpu.get_barrier_semaphore()
    for d in range(1, nx):
        pl.semaphore_signal(barrier, inc=1, device_id=along(d), device_id_type=MESH)
    for d in range(1, plane):
        pl.semaphore_signal(barrier, inc=1, device_id=across(d), device_id_type=MESH)

    loads = [
        pltpu.make_async_copy(source, target, load_sem.at[n])
        for n, (source, target) in enumerate((
            (flow, U.at[0, :, :, pl.ds(PAD, cz), :]),
            (cells_in, cells), (watch_in, watch), (blocks_in, blocks),
            (jac_in, jac), (table_in, table), (turns_in, turns), (history, held),
        ))
    ]
    for x in loads:
        x.start()

    there = [(index[axis] > 0, index[axis] < counts[axis] - 1) for axis in range(3)]

    def peer(axis, side):
        ids = list(index)
        ids[axis] = index[axis] + (1 if side else -1)
        return tuple(ids)

    for slot in range(3):
        for axis, buffer in enumerate((xr, zr, rr)):
            for side in range(2):
                @pl.when(jnp.logical_not(there[axis][side]))
                def _():
                    view = buffer.at[slot, side]
                    view[...] = jnp.zeros(view.shape, F32)

    def prepare():
        for x in loads[1:3]:
            x.wait()
        for i in range(cells.shape[0]):
            line[0:1, 64 * i:64 * i + 64] = cells[i:i + 1, :]
        for d in range(3):
            for g in range(observers // 128):
                wide = jnp.broadcast_to(watch[d:d + 1, g * 128:g * 128 + 128], (128, 128))
                columns = wide.T
                for n in range(128 // plane):
                    seats[d, pl.ds(g * (128 // plane) + n, plane, stride=nx), :] = columns[n * plane:(n + 1) * plane]

    lane = lax.broadcasted_iota(jnp.int32, (cz, cr), 1)
    lane8 = lax.broadcasted_iota(jnp.int32, (8, 128), 1)

    unit = 2.0 / grid[2]
    middle = 2.3
    norm = 1.0 / math.sqrt(nx * nz * nr * SURF_DEV)

    def geometry(i, carry):
        limit = blocks[0, 0] * 64
        span = pl.ds(pl.multiple_of(i * 32, 32), 32)
        at = (
            seats[0, span, :] * float(grid[0]),
            seats[1, span, :] * float(grid[1]),
            (1.25 + 0.75 * seats[2, span, :]) * float(grid[2]),
        )
        for g in range(groups):
            cols = slice(g * 128, (g + 1) * 128)
            spot = line[0:1, cols]
            place = (
                (index[0] * cx + spot // (cz * cr)).astype(F32) + 0.5,
                (index[1] * cz + spot // cr % cz).astype(F32) + 0.5,
                (index[2] * cr + spot % cr).astype(F32) + 0.5,
            )
            away = [at[d] - place[d] for d in range(3)]
            square = away[0] * away[0] + away[1] * away[1] + away[2] * away[2]
            distance = jnp.sqrt(square)
            inverse = 1.0 / distance
            for d in range(3):
                geo[d, span, cols] = away[d] * inverse
            geo[3, span, cols] = inverse * (1.0 / unit)
            angle = distance * unit - middle
            sq = angle * angle
            sine = angle * poly(sq, SIN)
            cosine = poly(sq, COS)
            cm, sm = math.cos(middle), math.sin(middle)
            step_r = cosine * cm - sine * sm
            step_i = -(sine * cm + cosine * sm)
            amp = jnp.where(lane + g * 128 < limit, inverse * (grid[2] * norm), 0.0)
            geo[4, span, cols] = step_r
            geo[5, span, cols] = step_i
            geo[6, span, cols] = amp * step_r
            geo[7, span, cols] = amp * step_i
        return carry

    def spectra():
        fourier = table[...]
        time = lax.broadcasted_iota(jnp.int32, fourier.shape, 1)
        early = jnp.where(time < times - STEPS, fourier, 0.0)
        for j in range(4):
            signal = held[j] + held[4] if j == 0 else held[j]
            spec[j] = lax.dot_general(
                early, signal, (((1,), (1,)), ((), ())),
                precision=lax.Precision.HIGHEST, preferred_element_type=F32,
            )

    def grow(step):
        at = times - STEPS + step
        for j in range(4):
            spec[j] = spec[j] + table[:, at:at + 1] * samples[step, j:j + 1, :]

    def turned(what, first):
        return (
            what * turns[first:first + 1, :]
            + pltpu.roll(what, 96, 1) * turns[first + 1:first + 2, :]
            + pltpu.roll(what, 32, 1) * turns[first + 2:first + 3, :]
        )

    def old_tile(i, carry):
        span = pl.ds(pl.multiple_of(i * 8, 8), 8)
        state = []
        for g in range(groups):
            state.append([geo[k, span, g * 128:(g + 1) * 128] for k in range(8)])
        result = jnp.zeros((8, 128), F32)
        for f in range(FREQ):
            real, imag = None, None
            for g in range(groups):
                cols = slice(g * 128, (g + 1) * 128)
                ex, ey, ez, near, zre, zim, ur, ui = state[g]
                tab[i, f, 0, :, cols] = ur
                tab[i, f, 1, :, cols] = ui
                sr = [spec[j, f:f + 1, cols] for j in range(4)]
                si = [spec[j, FREQ + f:FREQ + f + 1, cols] for j in range(4)]
                dr = ex * sr[1] + ey * sr[2] + ez * sr[3]
                di = ex * si[1] + ey * si[2] + ez * si[3]
                w = near * (1.0 / (f + 1))
                gr = w * dr - (si[0] + di)
                gi = w * di + (sr[0] + dr)
                pr = ur * gr - ui * gi
                pi = ur * gi + ui * gr
                real = pr if real is None else real + pr
                imag = pi if imag is None else imag + pi
                if f < FREQ - 1:
                    state[g][6] = ur * zre - ui * zim
                    state[g][7] = ur * zim + ui * zre
            result = jnp.where(lane8 == f, jnp.sum(real, axis=1, keepdims=True), result)
            result = jnp.where(lane8 == FREQ + f, jnp.sum(imag, axis=1, keepdims=True), result)
        value[span, :] = turned(result, 0)
        return carry

    def new_tile(i, t):
        span = pl.ds(pl.multiple_of(i * 8, 8), 8)
        weights = []
        for g in range(groups):
            cols = slice(g * 128, (g + 1) * 128)
            own = [samples[t, j:j + 1, cols] * (1.0 / math.sqrt(times)) for j in range(4)]
            dip = sum(geo[d, span, cols] * own[d + 1] for d in range(3))
            weights.append((own[0] + dip, geo[3, span, cols] * dip))
        what = jnp.zeros((8, 128), F32)
        for f in range(FREQ):
            phases = [[tab[i, f, n, :, g * 128:(g + 1) * 128] for n in range(2)] for g in range(groups)]
            for k in range(4):
                total = sum(weights[g][k // 2] * phases[g][k % 2] for g in range(groups))
                total = jnp.sum(total, axis=1, keepdims=True)
                what = jnp.where(lane8 == FREQ * k + f, total, what)
        return span, what

    def middle_tile(t, i, carry):
        span, what = new_tile(i, t)
        value[span, :] = value[span, :] + turned(what, 3 * (t + 1))
        return carry

    def last_tile(i, carry):
        span, what = new_tile(i, STEPS - 1)
        value[span, :] = value[span, :] + what
        return carry

    def fill(k):
        def upto(counts, i):
            return sum(jnp.where(i > n, count, 0) for n, count in enumerate(counts))

        for counts, act in (
            (OLD, old_tile), (NEW[0], functools.partial(middle_tile, 0)), (NEW[1], functools.partial(middle_tile, 1)),
        ):
            lax.fori_loop(upto(counts, k), upto(counts, k + 1), act, 0)

    def copy(axis, side, slot, mine):
        land = 1 - side if mine else side
        if axis == 0:
            src = U.at[slot, :, (cx - 1) if side else 0, pl.ds(PAD, cz), :]
            dst = xr.at[slot, land]
        elif axis == 1:
            src = zs.at[slot, side]
            dst = zr.at[slot, land]
        else:
            src = rs.at[slot]
            dst = rr.at[slot, land]
        return pltpu.make_async_remote_copy(
            src_ref=src, dst_ref=dst,
            send_sem=send_sem.at[axis, side, slot],
            recv_sem=recv_sem.at[axis, land, slot],
            device_id=peer(axis, side), device_id_type=MESH,
        )

    def for_sides(axis, act):
        for side in range(2):
            @pl.when(there[axis][side])
            def _():
                act(axis, side)

    def start_x(slot):
        for_sides(0, lambda axis, side: copy(axis, side, slot, True).start())

    def start_zr(slot):
        packed = jnp.zeros((cz, cr), F32)
        for v in range(NV):
            for x in range(cx):
                k = 2 * (v * cx + x)
                what = U[slot, v, x, PAD:PAD + cz, :]
                zs[slot, 0, v, x:x + 1, :] = what[:1]
                zs[slot, 1, v, x:x + 1, :] = what[cz - 1:]
                moved = pltpu.roll(what, k, 1) if k else what
                packed = jnp.where((lane == k) | (lane == (k - 1) % cr), moved, packed)
        rs[slot] = packed
        for axis in (2, 1):
            for_sides(axis, lambda axis, side: copy(axis, side, slot, True).start())

    def wait_received(axis, slot):
        for_sides(axis, lambda axis, side: copy(axis, side, slot, False).wait_recv())

    def wait_sent(slot):
        for axis in range(3):
            for_sides(axis, lambda axis, side: copy(axis, side, slot, True).wait_send())

    def pick(j, choices):
        return jnp.where(j == 0, choices[0], jnp.where(j == 1, choices[1], choices[2])).astype(F32)

    def stage(k):
        src, dst = lax.rem(k, 3), lax.rem(k + 1, 3)
        keep, gain = pick(src, KEEP), pick(src, GAIN)
        by_slope = gain * (0.5 * TIME_STEP)
        by_side = gain * (TIME_STEP * VISCOSITY)
        by_center = gain * (1.0 - 6.0 * VISCOSITY * TIME_STEP)
        for axis in (1, 2):
            wait_received(axis, src)
        for v in range(NV):
            for x in range(cx):
                U[src, v, x, PAD - 1:PAD, :] = zr[src, 0, v, x:x + 1, :]
                U[src, v, x, PAD + cz:PAD + cz + 1, :] = zr[src, 1, v, x:x + 1, :]
        halo = jnp.where(lane % 2 == 1, rr[src, 0], rr[src, 1])

        def layer(x):
            sums = [None] * NV
            rest = []
            for w in range(NV):
                center = U[src, w, x, PAD:PAD + cz, :]
                below = xr[src, 0, w] if x == 0 else U[src, w, x - 1, PAD:PAD + cz, :]
                above = xr[src, 1, w] if x == cx - 1 else U[src, w, x + 1, PAD:PAD + cz, :]
                before = U[src, w, x, PAD - 1:PAD + cz - 1, :]
                after = U[src, w, x, PAD + 1:PAD + cz + 1, :]
                n = 2 * (w * cx + x)
                moved = pltpu.roll(halo, cr - n, 1) if n else halo
                inner = pltpu.roll(jnp.where(lane == cr - 1, moved, center), 1, 1)
                outer = pltpu.roll(jnp.where(lane == 0, moved, center), cr - 1, 1)
                slopes = (above - below, after - before, outer - inner)
                beside = above + below + after + before + outer + inner
                rest.append(beside * by_side + center * by_center)
                for v in range(NV):
                    for d in range(3):
                        piece = slopes[d] * jac[v, d, w]
                        sums[v] = piece if sums[v] is None else sums[v] + piece
            for v in range(NV):
                what = sums[v] * by_slope + rest[v] + U[0, v, x, PAD:PAD + cz, :] * keep
                U[dst, v, x, PAD:PAD + cz, :] = what

        for x in range(1, cx - 1):
            layer(x)
        pl.when(there[0][0])(lambda: copy(0, 0, src, False).wait_recv())
        layer(0)
        pl.when((k < stages - 1) & there[0][0])(lambda: copy(0, 0, dst, True).start())
        pl.when(there[0][1])(lambda: copy(0, 1, src, False).wait_recv())
        layer(cx - 1)
        pl.when((k < stages - 1) & there[0][1])(lambda: copy(0, 1, dst, True).start())

    height = lax.broadcasted_iota(jnp.int32, (cr, slots), 0)
    rows_of = lax.broadcasted_iota(jnp.int32, (cx * cz, slots), 0)

    def sample(step):
        spot = line[...]
        chosen_lane = jnp.where(height == spot % cr, 1.0, 0.0).astype(jnp.bfloat16)
        for j in range(4):
            tile = jnp.concatenate([U[0, j, x, PAD:PAD + cz, :] for x in range(cx)], axis=0)
            if j == 0:
                tile = tile + jnp.concatenate([U[0, 4, x, PAD:PAD + cz, :] for x in range(cx)], axis=0)
            picked = split_dot(tile, chosen_lane)
            picked = jnp.where(rows_of == spot // cr, picked, 0.0)
            picked = jnp.sum(picked, axis=0, keepdims=True)
            samples[step, j:j + 1, :] = picked

    loads[0].wait()
    pl.semaphore_wait(barrier, nx - 1 + plane - 1)
    start_x(0)

    def body(k, carry):
        slot = lax.rem(k, 3)
        start_zr(slot)

        @pl.when(k == 0)
        def _():
            prepare()
            for x in loads[3:]:
                x.wait()
            lax.fori_loop(0, observers // 32, geometry, 0)
            spectra()

        for step in range(STEPS - 1):
            @pl.when(k == 3 * step + 3)
            def _():
                sample(step)
                grow(step)

        fill(k)
        stage(k)
        wait_sent(slot)
        return carry

    lax.fori_loop(0, stages, body, 0)
    result = pltpu.make_async_copy(U.at[0, :, :, pl.ds(PAD, cz), :], field, load_sem.at[0])
    result.start()
    sample(STEPS - 1)

    def first(d):
        to = lax.rem(seat + d, plane)
        return pltpu.make_async_remote_copy(
            src_ref=value.at[pl.ds(pl.multiple_of(to * nx, nx), nx)],
            dst_ref=got.at[d - 1], send_sem=send1.at[0], recv_sem=recv1.at[0],
            device_id=across(d), device_id_type=MESH,
        )

    def second(d):
        to = lax.rem(a + d, nx)
        return pltpu.make_async_remote_copy(
            src_ref=rows.at[to], dst_ref=last.at[d - 1],
            send_sem=send2.at[d - 1], recv_sem=recv2.at[d - 1],
            device_id=along(d), device_id_type=MESH,
        )

    def chunk(n, carry):
        pair = (2 * n + 1, 2 * n + 2)
        for d in pair:
            last_tile(lax.rem(seat + d, plane), 0)
        first(pair[0]).start()
        pl.when(pair[1] < plane)(lambda: first(pair[1]).start())
        return carry

    lax.fori_loop(0, plane // 2, chunk, 0)
    total = value[pl.ds(pl.multiple_of(seat * nx, nx), nx)]
    everything = pltpu.make_async_remote_copy(
        src_ref=got, dst_ref=got, send_sem=send1.at[0], recv_sem=recv1.at[0],
        device_id=across(1), device_id_type=MESH,
    )
    everything.wait_recv()
    total = total + jnp.sum(got[...], axis=0)
    rows[...] = total[:, None, :]
    for d in range(1, nx):
        second(d).start()
    for d in range(1, nx):
        second(d).wait_recv()
    total = rows[a] + jnp.sum(last[...], axis=0)
    spectrum = total * turns[9:10, :]
    for n, shift in enumerate((96, 64, 32)):
        spectrum = spectrum + pltpu.roll(total, shift, 1) * turns[10 + n:11 + n, :]
    out[...] = spectrum[:, :2 * FREQ]
    everything.wait_send()
    for d in range(1, nx):
        second(d).wait_send()
    result.wait()


def finish_kernel(field_in, spectrum_in, field, spectrum, held, line, sem):
    pairs = [(field_in.at[v], held.at[v], field.at[v]) for v in range(NV)]
    pairs.append((spectrum_in, line, spectrum))
    into = [pltpu.make_async_copy(p[0], p[1], sem.at[0, n]) for n, p in enumerate(pairs)]
    back = [pltpu.make_async_copy(p[1], p[2], sem.at[1, n]) for n, p in enumerate(pairs)]
    for x in into:
        x.start()
    for x, y in zip(into, back):
        x.wait()
        y.start()
    for y in back:
        y.wait()


def finish(field, spectrum):
    hbm = pl.BlockSpec(memory_space=pltpu.HBM)
    return pl.pallas_call(
        finish_kernel,
        out_shape=(
            jax.ShapeDtypeStruct(field.shape, F32),
            jax.ShapeDtypeStruct(spectrum.shape, F32),
        ),
        in_specs=[hbm, hbm],
        out_specs=(hbm, hbm),
        scratch_shapes=[
            pltpu.VMEM(field.shape, F32),
            pltpu.VMEM(spectrum.shape, F32),
            pltpu.SemaphoreType.DMA((2, NV + 1)),
        ],
        compiler_params=pltpu.CompilerParams(vmem_limit_bytes=63 << 20),
        name="finish",
    )(field, spectrum)


def solution(mesh):
    counts = tuple(mesh.shape[a] for a in AXES)
    nx, nz, nr = counts
    plane = nz * nr
    assert nx == 8 and plane == 32

    def per_device(flow, jacobian, history, cell, blocks, observers):
        sizes = counts + flow.shape[1:]
        cx, cz, cr = flow.shape[1:]
        slots, times = history.shape[0], history.shape[2]
        seats = observers.shape[1]
        hbm = pl.BlockSpec(memory_space=pltpu.HBM)
        dma = pltpu.SemaphoreType.DMA
        lanes = turn_rows(times)
        field, spectrum = pl.pallas_call(
            functools.partial(whole_kernel, sizes),
            out_shape=(
                jax.ShapeDtypeStruct(flow.shape, F32),
                jax.ShapeDtypeStruct((1, 2 * FREQ), F32),
            ),
            in_specs=[hbm] * 8,
            out_specs=(hbm, pl.BlockSpec(memory_space=pltpu.VMEM)),
            scratch_shapes=[
                pltpu.VMEM((3, NV, cx, cz + 2 * PAD, cr), F32),
                pltpu.VMEM(cell.shape, jnp.int32),
                pltpu.VMEM(observers.shape, F32),
                pltpu.SMEM(blocks.shape, jnp.int32),
                pltpu.SMEM((NV, 3, NV), F32),
                pltpu.VMEM((2 * FREQ, times), F32),
                pltpu.VMEM(lanes.shape, F32),
                pltpu.VMEM((NV, slots, times), F32),
                pltpu.VMEM((3, 2, NV, cz, cr), F32),
                pltpu.VMEM((3, 2, NV, cx, cr), F32),
                pltpu.VMEM((3, 2, NV, cx, cr), F32),
                pltpu.VMEM((3, cz, cr), F32),
                pltpu.VMEM((3, 2, cz, cr), F32),
                pltpu.VMEM((4, 2 * FREQ, slots), F32),
                pltpu.VMEM((STEPS, 8, slots), F32),
                pltpu.VMEM((8, seats, slots), F32),
                pltpu.VMEM((seats // 8, FREQ, 2, 8, slots), F32),
                pltpu.VMEM((3, seats, 128), F32),
                pltpu.VMEM((1, slots), jnp.int32),
                pltpu.VMEM((seats, 128), F32),
                pltpu.VMEM((plane - 1, nx, 128), F32),
                pltpu.VMEM((nx, 1, 128), F32),
                pltpu.VMEM((nx - 1, 1, 128), F32),
                dma((8,)),
                dma((3, 2, 3)),
                dma((3, 2, 3)),
                dma((1,)),
                dma((1,)),
                dma((nx - 1,)),
                dma((nx - 1,)),
            ],
            compiler_params=pltpu.CompilerParams(
                collective_id=0, has_side_effects=True, vmem_limit_bytes=63 << 20
            ),
            name="whole",
        )(
            flow, cell, observers, blocks, jacobian.transpose(1, 0, 2),
            jnp.asarray(fourier_table(times)), jnp.asarray(lanes), history.transpose(1, 0, 2),
        )
        return finish(field, spectrum)

    return jax.shard_map(
        per_device,
        mesh=mesh,
        in_specs=(
            P(None, "gx", "gz", "row"),
            P(),
            P(AXES, None, None),
            P(AXES, None),
            P("row", ("gx", "gz")),
            P(),
        ),
        out_specs=(P(None, "gx", "gz", "row"), P(AXES, None)),
        check_vma=False,
    )
```

```python
import functools
import math

import jax
import jax.numpy as jnp
import numpy as np
from jax import lax
from jax.experimental import pallas as pl
from jax.experimental.pallas import tpu as pltpu
from jax.sharding import PartitionSpec as P

F32 = jnp.float32
MESH = pl.DeviceIdType.MESH
NV = 5
FREQ = 32
STEPS = 3
SURF_DEV = 128
TIME_STEP = 0.3
VISCOSITY = 0.05
PAD = 8
KEEP = (0.0, 0.75, 1.0 / 3.0)
GAIN = (1.0, 0.25, 2.0 / 3.0)
AXES = ("gx", "gz", "row")
OLD = (0, 5, 5, 4, 4, 4, 3, 3, 4)
NEW = ((0, 0, 0, 2, 4, 4, 0, 0, 0), (0, 0, 0, 0, 0, 0, 7, 8, 7))


def split_dot(left, right):
    total = None
    for _ in range(3):
        part = left.astype(jnp.bfloat16)
        left = left - part.astype(F32)
        piece = jnp.dot(part, right, preferred_element_type=F32)
        total = piece if total is None else total + piece
    return total


def poly(x, coefficients):
    total = jnp.full_like(x, coefficients[-1])
    for c in coefficients[-2::-1]:
        total = total * x + c
    return total


SIN = [(-1.0) ** n / math.factorial(2 * n + 1) for n in range(9)]
COS = [(-1.0) ** n / math.factorial(2 * n) for n in range(10)]


def fourier_table(samples):
    turns = np.arange(1, FREQ + 1)[:, None] * np.arange(samples)[None, :] % samples
    angles = 2.0 * np.pi * turns / samples
    return (np.concatenate([np.cos(angles), -np.sin(angles)]) / np.sqrt(samples)).astype(np.float32)


def turn_rows(samples):
    f = np.arange(1, FREQ + 1)
    zero = np.zeros(FREQ)

    def turned(factor, both):
        re, im = factor.real, factor.imag
        return [
            np.concatenate([re, re, re, re] if both else [re, re, zero, zero]),
            np.concatenate([-im, zero, -im, zero] if both else [-im, zero, zero, zero]),
            np.concatenate([zero, im, zero, im] if both else [zero, im, zero, zero]),
        ]

    last = samples - 1
    rows = turned(-1j * np.exp(2j * np.pi * f * last / samples), False)
    for t in range(STEPS - 1):
        rows += turned(np.exp(2j * np.pi * f * (STEPS - 1 - t) / samples), True)
    w = np.exp(-2j * np.pi * f * last / samples)
    rows += [
        np.concatenate([-w.imag, -w.imag, zero, zero]),
        np.concatenate([-w.real, w.imag / f, zero, zero]),
        np.concatenate([w.real / f, w.real / f, zero, zero]),
        np.concatenate([-w.imag / f, w.real, zero, zero]),
    ]
    rows += [np.zeros(128)] * (-len(rows) % 8)
    return np.stack(rows).astype(np.float32)


def whole_kernel(
    sizes, flow, cells_in, watch_in, blocks_in, jac_in, table_in, turns_in, history, field, out,
    U, owed, cells, watch, blocks, jac, table, turns, held,
    xs, xr, zs, zr, rs, rr, spec, samples, geo, tab, seats, line, value, got, rows, last,
    load_sem, send_sem, recv_sem, send1, recv1, send2, recv2,
):
    nx, nz, nr, cx, cz, cr = sizes
    grid = (nx * cx, nz * cz, nr * cr)
    plane = nz * nr
    slots = line.shape[1]
    groups = slots // 128
    times = held.shape[2]
    observers = watch.shape[1]
    tiles = observers // 8
    stages = 3 * STEPS
    index = [lax.axis_index(a) for a in AXES]
    counts = (nx, nz, nr)
    a, b, c = index
    seat = b * nr + c

    def along(d):
        return (lax.rem(a + d, nx), b, c)

    def across(d):
        other = lax.rem(seat + d, plane)
        return (a, other // nr, lax.rem(other, nr))

    barrier = pltpu.get_barrier_semaphore()
    for d in range(1, nx):
        pl.semaphore_signal(barrier, inc=1, device_id=along(d), device_id_type=MESH)
    for d in range(1, plane):
        pl.semaphore_signal(barrier, inc=1, device_id=across(d), device_id_type=MESH)

    loads = [
        pltpu.make_async_copy(source, target, load_sem.at[n])
        for n, (source, target) in enumerate((
            (flow, U.at[0, :, :, pl.ds(PAD, cz), :]),
            (cells_in, cells), (watch_in, watch), (blocks_in, blocks),
            (jac_in, jac), (table_in, table), (turns_in, turns), (history, held),
        ))
    ]
    for x in loads:
        x.start()

    there = [(index[axis] > 0, index[axis] < counts[axis] - 1) for axis in range(3)]

    def peer(axis, side):
        ids = list(index)
        ids[axis] = index[axis] + (1 if side else -1)
        return tuple(ids)

    owed[...] = jnp.zeros(owed.shape, F32)
    for axis, buffer in enumerate((xr, zr, rr)):
        for slot in range(buffer.shape[0]):
            for side in range(2):
                @pl.when(jnp.logical_not(there[axis][side]))
                def _():
                    view = buffer.at[slot, side]
                    view[...] = jnp.zeros(view.shape, F32)

    def prepare():
        for x in loads[1:3]:
            x.wait()
        for i in range(cells.shape[0]):
            line[0:1, 64 * i:64 * i + 64] = cells[i:i + 1, :]
        for d in range(3):
            for g in range(observers // 128):
                wide = jnp.broadcast_to(watch[d:d + 1, g * 128:g * 128 + 128], (128, 128))
                columns = wide.T
                for n in range(128 // plane):
                    seats[d, pl.ds(g * (128 // plane) + n, plane, stride=nx), :] = columns[n * plane:(n + 1) * plane]

    lane = lax.broadcasted_iota(jnp.int32, (cz, cr), 1)
    lane8 = lax.broadcasted_iota(jnp.int32, (8, 128), 1)

    unit = 2.0 / grid[2]
    middle = 2.3
    norm = 1.0 / math.sqrt(nx * nz * nr * SURF_DEV)

    def geometry(i, carry):
        limit = blocks[0, 0] * 64
        span = pl.ds(pl.multiple_of(i * 32, 32), 32)
        at = (
            seats[0, span, :] * float(grid[0]),
            seats[1, span, :] * float(grid[1]),
            (1.25 + 0.75 * seats[2, span, :]) * float(grid[2]),
        )
        for g in range(groups):
            cols = slice(g * 128, (g + 1) * 128)
            spot = line[0:1, cols]
            place = (
                (index[0] * cx + spot // (cz * cr)).astype(F32) + 0.5,
                (index[1] * cz + spot // cr % cz).astype(F32) + 0.5,
                (index[2] * cr + spot % cr).astype(F32) + 0.5,
            )
            away = [at[d] - place[d] for d in range(3)]
            square = away[0] * away[0] + away[1] * away[1] + away[2] * away[2]
            distance = jnp.sqrt(square)
            inverse = 1.0 / distance
            for d in range(3):
                geo[d, span, cols] = away[d] * inverse
            geo[3, span, cols] = inverse * (1.0 / unit)
            angle = distance * unit - middle
            sq = angle * angle
            sine = angle * poly(sq, SIN)
            cosine = poly(sq, COS)
            cm, sm = math.cos(middle), math.sin(middle)
            step_r = cosine * cm - sine * sm
            step_i = -(sine * cm + cosine * sm)
            amp = jnp.where(lane + g * 128 < limit, inverse * (grid[2] * norm), 0.0)
            geo[4, span, cols] = step_r
            geo[5, span, cols] = step_i
            geo[6, span, cols] = amp * step_r
            geo[7, span, cols] = amp * step_i
        return carry

    def spectra():
        fourier = table[...]
        time = lax.broadcasted_iota(jnp.int32, fourier.shape, 1)
        early = jnp.where(time < times - STEPS, fourier, 0.0)
        for j in range(4):
            signal = held[j] + held[4] if j == 0 else held[j]
            spec[j] = lax.dot_general(
                early, signal, (((1,), (1,)), ((), ())),
                precision=lax.Precision.HIGHEST, preferred_element_type=F32,
            )

    def grow(step):
        at = times - STEPS + step
        for j in range(4):
            spec[j] = spec[j] + table[:, at:at + 1] * samples[step, j:j + 1, :]

    def turned(what, first):
        return (
            what * turns[first:first + 1, :]
            + pltpu.roll(what, 96, 1) * turns[first + 1:first + 2, :]
            + pltpu.roll(what, 32, 1) * turns[first + 2:first + 3, :]
        )

    def old_tile(i, carry):
        span = pl.ds(pl.multiple_of(i * 8, 8), 8)
        state = []
        for g in range(groups):
            state.append([geo[k, span, g * 128:(g + 1) * 128] for k in range(8)])
        result = jnp.zeros((8, 128), F32)
        for f in range(FREQ):
            real, imag = None, None
            for g in range(groups):
                cols = slice(g * 128, (g + 1) * 128)
                ex, ey, ez, near, zre, zim, ur, ui = state[g]
                tab[i, f, 0, :, cols] = ur
                tab[i, f, 1, :, cols] = ui
                sr = [spec[j, f:f + 1, cols] for j in range(4)]
                si = [spec[j, FREQ + f:FREQ + f + 1, cols] for j in range(4)]
                dr = ex * sr[1] + ey * sr[2] + ez * sr[3]
                di = ex * si[1] + ey * si[2] + ez * si[3]
                w = near * (1.0 / (f + 1))
                gr = w * dr - (si[0] + di)
                gi = w * di + (sr[0] + dr)
                pr = ur * gr - ui * gi
                pi = ur * gi + ui * gr
                real = pr if real is None else real + pr
                imag = pi if imag is None else imag + pi
                if f < FREQ - 1:
                    state[g][6] = ur * zre - ui * zim
                    state[g][7] = ur * zim + ui * zre
            result = jnp.where(lane8 == f, jnp.sum(real, axis=1, keepdims=True), result)
            result = jnp.where(lane8 == FREQ + f, jnp.sum(imag, axis=1, keepdims=True), result)
        value[span, :] = turned(result, 0)
        return carry

    def new_tile(i, t):
        span = pl.ds(pl.multiple_of(i * 8, 8), 8)
        weights = []
        for g in range(groups):
            cols = slice(g * 128, (g + 1) * 128)
            own = [samples[t, j:j + 1, cols] * (1.0 / math.sqrt(times)) for j in range(4)]
            dip = sum(geo[d, span, cols] * own[d + 1] for d in range(3))
            weights.append((own[0] + dip, geo[3, span, cols] * dip))
        what = jnp.zeros((8, 128), F32)
        for f in range(FREQ):
            phases = [[tab[i, f, n, :, g * 128:(g + 1) * 128] for n in range(2)] for g in range(groups)]
            for k in range(4):
                total = sum(weights[g][k // 2] * phases[g][k % 2] for g in range(groups))
                total = jnp.sum(total, axis=1, keepdims=True)
                what = jnp.where(lane8 == FREQ * k + f, total, what)
        return span, what

    def middle_tile(t, i, carry):
        span, what = new_tile(i, t)
        value[span, :] = value[span, :] + turned(what, 3 * (t + 1))
        return carry

    def last_tile(i, carry):
        span, what = new_tile(i, STEPS - 1)
        value[span, :] = value[span, :] + what
        return carry

    def fill(k):
        def upto(counts, i):
            return sum(jnp.where(i > n, count, 0) for n, count in enumerate(counts))

        for counts, act in (
            (OLD, old_tile), (NEW[0], functools.partial(middle_tile, 0)), (NEW[1], functools.partial(middle_tile, 1)),
        ):
            lax.fori_loop(upto(counts, k), upto(counts, k + 1), act, 0)

    def copy(axis, side, slot, mine):
        land = 1 - side if mine else side
        if axis == 0:
            src = xs.at[slot, side]
            dst = xr.at[slot, land]
        elif axis == 1:
            src = zs.at[slot, side]
            dst = zr.at[slot, land]
        else:
            src = rs.at[slot]
            dst = rr.at[slot, land]
        return pltpu.make_async_remote_copy(
            src_ref=src, dst_ref=dst,
            send_sem=send_sem.at[axis, side, slot],
            recv_sem=recv_sem.at[axis, land, slot],
            device_id=peer(axis, side), device_id_type=MESH,
        )

    def for_sides(axis, act):
        for side in range(2):
            @pl.when(there[axis][side])
            def _():
                act(axis, side)

    def start_x(slot):
        for_sides(0, lambda axis, side: copy(axis, side, slot, True).start())

    def start_zr(slot):
        packed = jnp.zeros((cz, cr), F32)
        for v in range(NV):
            for x in range(cx):
                k = 2 * (v * cx + x)
                what = U[slot, v, x, PAD:PAD + cz, :]
                zs[slot, 0, v, x:x + 1, :] = what[:1]
                zs[slot, 1, v, x:x + 1, :] = what[cz - 1:]
                moved = pltpu.roll(what, k, 1) if k else what
                packed = jnp.where((lane == k) | (lane == (k - 1) % cr), moved, packed)
        rs[slot] = packed
        for axis in (2, 1):
            for_sides(axis, lambda axis, side: copy(axis, side, slot, True).start())

    def wait_received(axis, slot):
        for_sides(axis, lambda axis, side: copy(axis, side, slot, False).wait_recv())

    def wait_sent(k):
        for axis in range(3):
            slot = lax.rem(k, 3 if axis else 4)
            for_sides(axis, lambda axis, side: copy(axis, side, slot, True).wait_send())

    def pick(j, choices):
        return jnp.where(j == 0, choices[0], jnp.where(j == 1, choices[1], choices[2])).astype(F32)

    def stage(k):
        src, dst = lax.rem(k, 3), lax.rem(k + 1, 3)
        xsrc, xdst = lax.rem(k, 4), lax.rem(k + 1, 4)
        keep, gain = pick(src, KEEP), pick(src, GAIN)
        by_slope = gain * (0.5 * TIME_STEP)
        by_side = gain * (TIME_STEP * VISCOSITY)
        by_center = gain * (1.0 - 6.0 * VISCOSITY * TIME_STEP)
        def across_face(values, side, slope, level):
            added = []
            for v in range(NV):
                total = sum(values[w] * jac[v, 0, w] for w in range(NV)) * slope
                added.append(values[v] * level + total if side else values[v] * level - total)
            return added

        old = lax.rem(k + 2, 3)
        old_gain = pick(old, GAIN)
        for side, x in ((0, 0), (1, cx - 1)):
            @pl.when(there[0][side] & (k > 0))
            def _():
                mine = [U[old, w, x, PAD:PAD + cz, :] for w in range(NV)]
                added = across_face(mine, 1 - side, old_gain * (0.5 * TIME_STEP), old_gain * (TIME_STEP * VISCOSITY))
                for v in range(NV):
                    owed[side, v] = added[v]

        for axis in (1, 2):
            wait_received(axis, src)
        for v in range(NV):
            for x in range(cx):
                U[src, v, x, PAD - 1:PAD, :] = zr[src, 0, v, x:x + 1, :]
                U[src, v, x, PAD + cz:PAD + cz + 1, :] = zr[src, 1, v, x:x + 1, :]
        halo = jnp.where(lane % 2 == 1, rr[src, 0], rr[src, 1])

        def layer(x):
            sums = [None] * NV
            rest = []
            for w in range(NV):
                center = U[src, w, x, PAD:PAD + cz, :]
                below = None if x == 0 else U[src, w, x - 1, PAD:PAD + cz, :]
                above = None if x == cx - 1 else U[src, w, x + 1, PAD:PAD + cz, :]
                before = U[src, w, x, PAD - 1:PAD + cz - 1, :]
                after = U[src, w, x, PAD + 1:PAD + cz + 1, :]
                n = 2 * (w * cx + x)
                moved = pltpu.roll(halo, cr - n, 1) if n else halo
                inner = pltpu.roll(jnp.where(lane == cr - 1, moved, center), 1, 1)
                outer = pltpu.roll(jnp.where(lane == 0, moved, center), cr - 1, 1)
                if below is None:
                    slope, both = above, above
                elif above is None:
                    slope, both = -below, below
                else:
                    slope, both = above - below, above + below
                slopes = (slope, after - before, outer - inner)
                beside = both + after + before + outer + inner
                rest.append(beside * by_side + center * by_center)
                for v in range(NV):
                    for d in range(3):
                        piece = slopes[d] * jac[v, d, w]
                        sums[v] = piece if sums[v] is None else sums[v] + piece
            for v in range(NV):
                what = sums[v] * by_slope + rest[v] + U[0, v, x, PAD:PAD + cz, :] * keep
                if x == 0:
                    xs[xdst, 0, v] = what
                elif x == cx - 1:
                    xs[xdst, 1, v] = what
                else:
                    U[dst, v, x, PAD:PAD + cz, :] = what

        for side, x in ((0, 0), (1, cx - 1)):
            layer(x)
            pl.when((k < stages - 1) & there[0][side])(lambda: copy(0, side, xdst, True).start())
        for x in range(1, cx - 1):
            layer(x)
        for side, x in ((0, 0), (1, cx - 1)):
            pl.when(there[0][side])(lambda: copy(0, side, xsrc, False).wait_recv())
            theirs = [xr[xsrc, side, w] + owed[side, w] for w in range(NV)]
            added = across_face(theirs, side, by_slope, by_side)
            for v in range(NV):
                U[dst, v, x, PAD:PAD + cz, :] = xs[xdst, side, v] + added[v]

    height = lax.broadcasted_iota(jnp.int32, (cr, slots), 0)
    rows_of = lax.broadcasted_iota(jnp.int32, (cx * cz, slots), 0)

    def sample(step):
        spot = line[...]
        chosen_lane = jnp.where(height == spot % cr, 1.0, 0.0).astype(jnp.bfloat16)
        for j in range(4):
            tile = jnp.concatenate([U[0, j, x, PAD:PAD + cz, :] for x in range(cx)], axis=0)
            if j == 0:
                tile = tile + jnp.concatenate([U[0, 4, x, PAD:PAD + cz, :] for x in range(cx)], axis=0)
            picked = split_dot(tile, chosen_lane)
            picked = jnp.where(rows_of == spot // cr, picked, 0.0)
            picked = jnp.sum(picked, axis=0, keepdims=True)
            samples[step, j:j + 1, :] = picked

    loads[0].wait()
    pl.semaphore_wait(barrier, nx - 1 + plane - 1)
    for side in range(2):
        xs[0, side] = U[0, :, (cx - 1) * side, PAD:PAD + cz, :]
    start_x(0)

    def body(k, carry):
        slot = lax.rem(k, 3)
        start_zr(slot)

        @pl.when(k == 0)
        def _():
            prepare()
            for x in loads[3:]:
                x.wait()
            lax.fori_loop(0, observers // 32, geometry, 0)
            spectra()

        for step in range(STEPS - 1):
            @pl.when(k == 3 * step + 3)
            def _():
                sample(step)
                grow(step)

        fill(k)
        stage(k)
        wait_sent(k)
        return carry

    lax.fori_loop(0, stages, body, 0)
    result = pltpu.make_async_copy(U.at[0, :, :, pl.ds(PAD, cz), :], field, load_sem.at[0])
    result.start()
    sample(STEPS - 1)

    def first(d):
        to = lax.rem(seat + d, plane)
        return pltpu.make_async_remote_copy(
            src_ref=value.at[pl.ds(pl.multiple_of(to * nx, nx), nx)],
            dst_ref=got.at[d - 1], send_sem=send1.at[0], recv_sem=recv1.at[0],
            device_id=across(d), device_id_type=MESH,
        )

    def second(d):
        to = lax.rem(a + d, nx)
        return pltpu.make_async_remote_copy(
            src_ref=rows.at[to], dst_ref=last.at[d - 1],
            send_sem=send2.at[d - 1], recv_sem=recv2.at[d - 1],
            device_id=along(d), device_id_type=MESH,
        )

    def chunk(n, carry):
        pair = (2 * n + 1, 2 * n + 2)
        for d in pair:
            last_tile(lax.rem(seat + d, plane), 0)
        first(pair[0]).start()
        pl.when(pair[1] < plane)(lambda: first(pair[1]).start())
        return carry

    lax.fori_loop(0, plane // 2, chunk, 0)
    total = value[pl.ds(pl.multiple_of(seat * nx, nx), nx)]
    everything = pltpu.make_async_remote_copy(
        src_ref=got, dst_ref=got, send_sem=send1.at[0], recv_sem=recv1.at[0],
        device_id=across(1), device_id_type=MESH,
    )
    everything.wait_recv()
    total = total + jnp.sum(got[...], axis=0)
    rows[...] = total[:, None, :]
    for d in range(1, nx):
        second(d).start()
    for d in range(1, nx):
        second(d).wait_recv()
    total = rows[a] + jnp.sum(last[...], axis=0)
    spectrum = total * turns[9:10, :]
    for n, shift in enumerate((96, 64, 32)):
        spectrum = spectrum + pltpu.roll(total, shift, 1) * turns[10 + n:11 + n, :]
    out[...] = spectrum[:, :2 * FREQ]
    everything.wait_send()
    for d in range(1, nx):
        second(d).wait_send()
    result.wait()


def finish_kernel(field_in, spectrum_in, field, spectrum, held, line, sem):
    pairs = [(field_in.at[v], held.at[v], field.at[v]) for v in range(NV)]
    pairs.append((spectrum_in, line, spectrum))
    into = [pltpu.make_async_copy(p[0], p[1], sem.at[0, n]) for n, p in enumerate(pairs)]
    back = [pltpu.make_async_copy(p[1], p[2], sem.at[1, n]) for n, p in enumerate(pairs)]
    for x in into:
        x.start()
    for x, y in zip(into, back):
        x.wait()
        y.start()
    for y in back:
        y.wait()


def finish(field, spectrum):
    hbm = pl.BlockSpec(memory_space=pltpu.HBM)
    return pl.pallas_call(
        finish_kernel,
        out_shape=(
            jax.ShapeDtypeStruct(field.shape, F32),
            jax.ShapeDtypeStruct(spectrum.shape, F32),
        ),
        in_specs=[hbm, hbm],
        out_specs=(hbm, hbm),
        scratch_shapes=[
            pltpu.VMEM(field.shape, F32),
            pltpu.VMEM(spectrum.shape, F32),
            pltpu.SemaphoreType.DMA((2, NV + 1)),
        ],
        compiler_params=pltpu.CompilerParams(vmem_limit_bytes=63 << 20),
        name="finish",
    )(field, spectrum)


def solution(mesh):
    counts = tuple(mesh.shape[a] for a in AXES)
    nx, nz, nr = counts
    plane = nz * nr
    assert nx == 8 and plane == 32

    def per_device(flow, jacobian, history, cell, blocks, observers):
        sizes = counts + flow.shape[1:]
        cx, cz, cr = flow.shape[1:]
        slots, times = history.shape[0], history.shape[2]
        seats = observers.shape[1]
        hbm = pl.BlockSpec(memory_space=pltpu.HBM)
        dma = pltpu.SemaphoreType.DMA
        lanes = turn_rows(times)
        field, spectrum = pl.pallas_call(
            functools.partial(whole_kernel, sizes),
            out_shape=(
                jax.ShapeDtypeStruct(flow.shape, F32),
                jax.ShapeDtypeStruct((1, 2 * FREQ), F32),
            ),
            in_specs=[hbm] * 8,
            out_specs=(hbm, pl.BlockSpec(memory_space=pltpu.VMEM)),
            scratch_shapes=[
                pltpu.VMEM((3, NV, cx, cz + 2 * PAD, cr), F32),
                pltpu.VMEM((2, NV, cz, cr), F32),
                pltpu.VMEM(cell.shape, jnp.int32),
                pltpu.VMEM(observers.shape, F32),
                pltpu.SMEM(blocks.shape, jnp.int32),
                pltpu.SMEM((NV, 3, NV), F32),
                pltpu.VMEM((2 * FREQ, times), F32),
                pltpu.VMEM(lanes.shape, F32),
                pltpu.VMEM((NV, slots, times), F32),
                pltpu.VMEM((4, 2, NV, cz, cr), F32),
                pltpu.VMEM((4, 2, NV, cz, cr), F32),
                pltpu.VMEM((3, 2, NV, cx, cr), F32),
                pltpu.VMEM((3, 2, NV, cx, cr), F32),
                pltpu.VMEM((3, cz, cr), F32),
                pltpu.VMEM((3, 2, cz, cr), F32),
                pltpu.VMEM((4, 2 * FREQ, slots), F32),
                pltpu.VMEM((STEPS, 8, slots), F32),
                pltpu.VMEM((8, seats, slots), F32),
                pltpu.VMEM((seats // 8, FREQ, 2, 8, slots), F32),
                pltpu.VMEM((3, seats, 128), F32),
                pltpu.VMEM((1, slots), jnp.int32),
                pltpu.VMEM((seats, 128), F32),
                pltpu.VMEM((plane - 1, nx, 128), F32),
                pltpu.VMEM((nx, 1, 128), F32),
                pltpu.VMEM((nx - 1, 1, 128), F32),
                dma((8,)),
                dma((3, 2, 4)),
                dma((3, 2, 4)),
                dma((1,)),
                dma((1,)),
                dma((nx - 1,)),
                dma((nx - 1,)),
            ],
            compiler_params=pltpu.CompilerParams(
                collective_id=0, has_side_effects=True, vmem_limit_bytes=63 << 20
            ),
            name="whole",
        )(
            flow, cell, observers, blocks, jacobian.transpose(1, 0, 2),
            jnp.asarray(fourier_table(times)), jnp.asarray(lanes), history.transpose(1, 0, 2),
        )
        return finish(field, spectrum)

    return jax.shard_map(
        per_device,
        mesh=mesh,
        in_specs=(
            P(None, "gx", "gz", "row"),
            P(),
            P(AXES, None, None),
            P(AXES, None),
            P("row", ("gx", "gz")),
            P(),
        ),
        out_specs=(P(None, "gx", "gz", "row"), P(AXES, None)),
        check_vma=False,
    )
```

```python
import functools
import math

import jax
import jax.numpy as jnp
import numpy as np
from jax import lax
from jax.experimental import pallas as pl
from jax.experimental.pallas import tpu as pltpu
from jax.sharding import PartitionSpec as P

F32 = jnp.float32
MESH = pl.DeviceIdType.MESH
NV = 5
FREQ = 32
STEPS = 3
SURF_DEV = 128
TIME_STEP = 0.3
VISCOSITY = 0.05
PAD = 8
KEEP = (0.0, 0.75, 1.0 / 3.0)
GAIN = (1.0, 0.25, 2.0 / 3.0)
AXES = ("gx", "gz", "row")
OLD = (0, 5, 5, 4, 4, 4, 3, 3, 4)
NEW = ((0, 0, 0, 2, 4, 4, 0, 0, 0), (0, 0, 0, 0, 0, 0, 6, 8, 8))


def split_dot(left, right):
    total = None
    for _ in range(3):
        part = left.astype(jnp.bfloat16)
        left = left - part.astype(F32)
        piece = jnp.dot(part, right, preferred_element_type=F32)
        total = piece if total is None else total + piece
    return total


def poly(x, coefficients):
    total = jnp.full_like(x, coefficients[-1])
    for c in coefficients[-2::-1]:
        total = total * x + c
    return total


SIN = [(-1.0) ** n / math.factorial(2 * n + 1) for n in range(9)]
COS = [(-1.0) ** n / math.factorial(2 * n) for n in range(10)]


def fourier_table(samples):
    turns = np.arange(1, FREQ + 1)[:, None] * np.arange(samples)[None, :] % samples
    angles = 2.0 * np.pi * turns / samples
    return (np.concatenate([np.cos(angles), -np.sin(angles)]) / np.sqrt(samples)).astype(np.float32)


def turn_rows(samples):
    f = np.arange(1, FREQ + 1)
    zero = np.zeros(FREQ)

    def turned(factor, both):
        re, im = factor.real, factor.imag
        return [
            np.concatenate([re, re, re, re] if both else [re, re, zero, zero]),
            np.concatenate([-im, zero, -im, zero] if both else [-im, zero, zero, zero]),
            np.concatenate([zero, im, zero, im] if both else [zero, im, zero, zero]),
        ]

    last = samples - 1
    rows = turned(-1j * np.exp(2j * np.pi * f * last / samples), False)
    for t in range(STEPS - 1):
        rows += turned(np.exp(2j * np.pi * f * (STEPS - 1 - t) / samples), True)
    w = np.exp(-2j * np.pi * f * last / samples)
    rows += [
        np.concatenate([-w.imag, -w.imag, zero, zero]),
        np.concatenate([-w.real, w.imag / f, zero, zero]),
        np.concatenate([w.real / f, w.real / f, zero, zero]),
        np.concatenate([-w.imag / f, w.real, zero, zero]),
    ]
    rows += [np.zeros(128)] * (-len(rows) % 8)
    return np.stack(rows).astype(np.float32)


def whole_kernel(
    sizes, flow, cells_in, watch_in, blocks_in, jac_in, table_in, turns_in, history, field, out,
    U, owed, cells, watch, blocks, jac, table, turns, held,
    xs, xr, zs, zr, rs, rr, spec, samples, geo, tab, seats, line, value, got, rows, last,
    load_sem, send_sem, recv_sem, send1, recv1, send2, recv2,
):
    nx, nz, nr, cx, cz, cr = sizes
    grid = (nx * cx, nz * cz, nr * cr)
    plane = nz * nr
    slots = line.shape[1]
    groups = slots // 128
    times = held.shape[2]
    observers = watch.shape[1]
    tiles = observers // 8
    stages = 3 * STEPS
    index = [lax.axis_index(a) for a in AXES]
    counts = (nx, nz, nr)
    a, b, c = index
    seat = b * nr + c

    def along(d):
        return (lax.rem(a + d, nx), b, c)

    def across(d):
        other = lax.rem(seat + d, plane)
        return (a, other // nr, lax.rem(other, nr))

    barrier = pltpu.get_barrier_semaphore()
    for d in range(1, nx):
        pl.semaphore_signal(barrier, inc=1, device_id=along(d), device_id_type=MESH)
    for d in range(1, plane):
        pl.semaphore_signal(barrier, inc=1, device_id=across(d), device_id_type=MESH)

    loads = [
        pltpu.make_async_copy(source, target, load_sem.at[n])
        for n, (source, target) in enumerate((
            (flow, U.at[0, :, :, pl.ds(PAD, cz), :]),
            (cells_in, cells), (watch_in, watch), (blocks_in, blocks),
            (jac_in, jac), (table_in, table), (turns_in, turns), (history, held),
        ))
    ]
    for x in loads:
        x.start()

    there = [(index[axis] > 0, index[axis] < counts[axis] - 1) for axis in range(3)]

    def peer(axis, side):
        ids = list(index)
        ids[axis] = index[axis] + (1 if side else -1)
        return tuple(ids)

    owed[...] = jnp.zeros(owed.shape, F32)
    for axis, buffer in enumerate((xr, zr, rr)):
        for slot in range(buffer.shape[0]):
            for side in range(2):
                @pl.when(jnp.logical_not(there[axis][side]))
                def _():
                    view = buffer.at[slot, side]
                    view[...] = jnp.zeros(view.shape, F32)

    def prepare():
        for x in loads[1:3]:
            x.wait()
        for i in range(cells.shape[0]):
            line[0:1, 64 * i:64 * i + 64] = cells[i:i + 1, :]
        for d in range(3):
            for g in range(observers // 128):
                wide = jnp.broadcast_to(watch[d:d + 1, g * 128:g * 128 + 128], (128, 128))
                columns = wide.T
                for n in range(128 // plane):
                    seats[d, pl.ds(g * (128 // plane) + n, plane, stride=nx), :] = columns[n * plane:(n + 1) * plane]

    lane = lax.broadcasted_iota(jnp.int32, (cz, cr), 1)
    lane8 = lax.broadcasted_iota(jnp.int32, (8, 128), 1)

    unit = 2.0 / grid[2]
    middle = 2.3
    norm = 1.0 / math.sqrt(nx * nz * nr * SURF_DEV)

    def geometry(i, carry):
        limit = blocks[0, 0] * 64
        span = pl.ds(pl.multiple_of(i * 32, 32), 32)
        at = (
            seats[0, span, :] * float(grid[0]),
            seats[1, span, :] * float(grid[1]),
            (1.25 + 0.75 * seats[2, span, :]) * float(grid[2]),
        )
        for g in range(groups):
            cols = slice(g * 128, (g + 1) * 128)
            spot = line[0:1, cols]
            place = (
                (index[0] * cx + spot // (cz * cr)).astype(F32) + 0.5,
                (index[1] * cz + spot // cr % cz).astype(F32) + 0.5,
                (index[2] * cr + spot % cr).astype(F32) + 0.5,
            )
            away = [at[d] - place[d] for d in range(3)]
            square = away[0] * away[0] + away[1] * away[1] + away[2] * away[2]
            distance = jnp.sqrt(square)
            inverse = 1.0 / distance
            for d in range(3):
                geo[d, span, cols] = away[d] * inverse
            geo[3, span, cols] = inverse * (1.0 / unit)
            angle = distance * unit - middle
            sq = angle * angle
            sine = angle * poly(sq, SIN)
            cosine = poly(sq, COS)
            cm, sm = math.cos(middle), math.sin(middle)
            step_r = cosine * cm - sine * sm
            step_i = -(sine * cm + cosine * sm)
            amp = jnp.where(lane + g * 128 < limit, inverse * (grid[2] * norm), 0.0)
            geo[4, span, cols] = step_r
            geo[5, span, cols] = step_i
            geo[6, span, cols] = amp * step_r
            geo[7, span, cols] = amp * step_i
        return carry

    def spectra():
        fourier = table[...]
        time = lax.broadcasted_iota(jnp.int32, fourier.shape, 1)
        early = jnp.where(time < times - STEPS, fourier, 0.0)
        for j in range(4):
            signal = held[j] + held[4] if j == 0 else held[j]
            spec[j] = lax.dot_general(
                early, signal, (((1,), (1,)), ((), ())),
                precision=lax.Precision.HIGHEST, preferred_element_type=F32,
            )

    def grow(step):
        at = times - STEPS + step
        for j in range(4):
            spec[j] = spec[j] + table[:, at:at + 1] * samples[step, j:j + 1, :]

    def turned(what, first):
        return (
            what * turns[first:first + 1, :]
            + pltpu.roll(what, 96, 1) * turns[first + 1:first + 2, :]
            + pltpu.roll(what, 32, 1) * turns[first + 2:first + 3, :]
        )

    def old_tile(i, carry):
        span = pl.ds(pl.multiple_of(i * 8, 8), 8)
        state = []
        for g in range(groups):
            state.append([geo[k, span, g * 128:(g + 1) * 128] for k in range(8)])
        result = jnp.zeros((8, 128), F32)
        for f in range(FREQ):
            real, imag = None, None
            for g in range(groups):
                cols = slice(g * 128, (g + 1) * 128)
                ex, ey, ez, near, zre, zim, ur, ui = state[g]
                tab[i, f, 0, :, cols] = ur
                tab[i, f, 1, :, cols] = ui
                sr = [spec[j, f:f + 1, cols] for j in range(4)]
                si = [spec[j, FREQ + f:FREQ + f + 1, cols] for j in range(4)]
                dr = ex * sr[1] + ey * sr[2] + ez * sr[3]
                di = ex * si[1] + ey * si[2] + ez * si[3]
                w = near * (1.0 / (f + 1))
                gr = w * dr - (si[0] + di)
                gi = w * di + (sr[0] + dr)
                pr = ur * gr - ui * gi
                pi = ur * gi + ui * gr
                real = pr if real is None else real + pr
                imag = pi if imag is None else imag + pi
                if f < FREQ - 1:
                    state[g][6] = ur * zre - ui * zim
                    state[g][7] = ur * zim + ui * zre
            result = jnp.where(lane8 == f, jnp.sum(real, axis=1, keepdims=True), result)
            result = jnp.where(lane8 == FREQ + f, jnp.sum(imag, axis=1, keepdims=True), result)
        value[span, :] = turned(result, 0)
        return carry

    def new_tile(i, t):
        span = pl.ds(pl.multiple_of(i * 8, 8), 8)
        weights = []
        for g in range(groups):
            cols = slice(g * 128, (g + 1) * 128)
            own = [samples[t, j:j + 1, cols] * (1.0 / math.sqrt(times)) for j in range(4)]
            dip = sum(geo[d, span, cols] * own[d + 1] for d in range(3))
            weights.append((own[0] + dip, geo[3, span, cols] * dip))
        what = jnp.zeros((8, 128), F32)
        for f in range(FREQ):
            phases = [[tab[i, f, n, :, g * 128:(g + 1) * 128] for n in range(2)] for g in range(groups)]
            for k in range(4):
                total = sum(weights[g][k // 2] * phases[g][k % 2] for g in range(groups))
                total = jnp.sum(total, axis=1, keepdims=True)
                what = jnp.where(lane8 == FREQ * k + f, total, what)
        return span, what

    def middle_tile(t, i, carry):
        span, what = new_tile(i, t)
        value[span, :] = value[span, :] + turned(what, 3 * (t + 1))
        return carry

    def last_tile(i, carry):
        span, what = new_tile(i, STEPS - 1)
        value[span, :] = value[span, :] + what
        return carry

    def middle_pair(t, n, carry):
        middle_tile(t, 2 * n, 0)
        middle_tile(t, 2 * n + 1, 0)
        return carry

    def fill(k):
        def upto(counts, i):
            return sum(jnp.where(i > n, count, 0) for n, count in enumerate(counts))

        lax.fori_loop(upto(OLD, k), upto(OLD, k + 1), old_tile, 0)
        for t in range(STEPS - 1):
            pairs = [count // 2 for count in NEW[t]]
            lax.fori_loop(upto(pairs, k), upto(pairs, k + 1), functools.partial(middle_pair, t), 0)

    def copy(axis, side, slot, mine):
        land = 1 - side if mine else side
        if axis == 0:
            src = xs.at[slot, side]
            dst = xr.at[slot, land]
        elif axis == 1:
            src = zs.at[slot, side]
            dst = zr.at[slot, land]
        else:
            src = rs.at[slot]
            dst = rr.at[slot, land]
        return pltpu.make_async_remote_copy(
            src_ref=src, dst_ref=dst,
            send_sem=send_sem.at[axis, side, slot],
            recv_sem=recv_sem.at[axis, land, slot],
            device_id=peer(axis, side), device_id_type=MESH,
        )

    def for_sides(axis, act):
        for side in range(2):
            @pl.when(there[axis][side])
            def _():
                act(axis, side)

    def start_x(slot):
        for_sides(0, lambda axis, side: copy(axis, side, slot, True).start())

    def start_zr(slot):
        packed = jnp.zeros((cz, cr), F32)
        for v in range(NV):
            for x in range(cx):
                k = 2 * (v * cx + x)
                what = U[slot, v, x, PAD:PAD + cz, :]
                zs[slot, 0, v, x:x + 1, :] = what[:1]
                zs[slot, 1, v, x:x + 1, :] = what[cz - 1:]
                moved = pltpu.roll(what, k, 1) if k else what
                packed = jnp.where((lane == k) | (lane == (k - 1) % cr), moved, packed)
        rs[slot] = packed
        for axis in (2, 1):
            for_sides(axis, lambda axis, side: copy(axis, side, slot, True).start())

    def wait_received(axis, slot):
        for_sides(axis, lambda axis, side: copy(axis, side, slot, False).wait_recv())

    def wait_sent(k):
        for axis in range(3):
            slot = lax.rem(k, 3 if axis else 4)
            for_sides(axis, lambda axis, side: copy(axis, side, slot, True).wait_send())

    def pick(j, choices):
        return jnp.where(j == 0, choices[0], jnp.where(j == 1, choices[1], choices[2])).astype(F32)

    def stage(k):
        src, dst = lax.rem(k, 3), lax.rem(k + 1, 3)
        xsrc, xdst = lax.rem(k, 4), lax.rem(k + 1, 4)
        keep, gain = pick(src, KEEP), pick(src, GAIN)
        by_slope = gain * (0.5 * TIME_STEP)
        by_side = gain * (TIME_STEP * VISCOSITY)
        by_center = gain * (1.0 - 6.0 * VISCOSITY * TIME_STEP)
        def across_face(values, side, slope, level):
            added = []
            for v in range(NV):
                total = sum(values[w] * jac[v, 0, w] for w in range(NV)) * slope
                added.append(values[v] * level + total if side else values[v] * level - total)
            return added

        old = lax.rem(k + 2, 3)
        old_gain = pick(old, GAIN)
        for side, x in ((0, 0), (1, cx - 1)):
            @pl.when(there[0][side] & (k > 0))
            def _():
                mine = [U[old, w, x, PAD:PAD + cz, :] for w in range(NV)]
                added = across_face(mine, 1 - side, old_gain * (0.5 * TIME_STEP), old_gain * (TIME_STEP * VISCOSITY))
                for v in range(NV):
                    owed[side, v] = added[v]

        for axis in (1, 2):
            wait_received(axis, src)
        for v in range(NV):
            for x in range(cx):
                U[src, v, x, PAD - 1:PAD, :] = zr[src, 0, v, x:x + 1, :]
                U[src, v, x, PAD + cz:PAD + cz + 1, :] = zr[src, 1, v, x:x + 1, :]
        halo = jnp.where(lane % 2 == 1, rr[src, 0], rr[src, 1])

        def layer(x):
            sums = [None] * NV
            rest = []
            for w in range(NV):
                center = U[src, w, x, PAD:PAD + cz, :]
                below = None if x == 0 else U[src, w, x - 1, PAD:PAD + cz, :]
                above = None if x == cx - 1 else U[src, w, x + 1, PAD:PAD + cz, :]
                before = U[src, w, x, PAD - 1:PAD + cz - 1, :]
                after = U[src, w, x, PAD + 1:PAD + cz + 1, :]
                n = 2 * (w * cx + x)
                moved = pltpu.roll(halo, cr - n, 1) if n else halo
                inner = pltpu.roll(jnp.where(lane == cr - 1, moved, center), 1, 1)
                outer = pltpu.roll(jnp.where(lane == 0, moved, center), cr - 1, 1)
                if below is None:
                    slope, both = above, above
                elif above is None:
                    slope, both = -below, below
                else:
                    slope, both = above - below, above + below
                slopes = (slope, after - before, outer - inner)
                beside = both + after + before + outer + inner
                rest.append(beside * by_side + center * by_center)
                for v in range(NV):
                    for d in range(3):
                        piece = slopes[d] * jac[v, d, w]
                        sums[v] = piece if sums[v] is None else sums[v] + piece
            for v in range(NV):
                what = sums[v] * by_slope + rest[v] + U[0, v, x, PAD:PAD + cz, :] * keep
                if x == 0:
                    xs[xdst, 0, v] = what
                elif x == cx - 1:
                    xs[xdst, 1, v] = what
                else:
                    U[dst, v, x, PAD:PAD + cz, :] = what

        for side, x in ((0, 0), (1, cx - 1)):
            layer(x)
            pl.when((k < stages - 1) & there[0][side])(lambda: copy(0, side, xdst, True).start())
        for x in range(1, cx - 1):
            layer(x)
        for side, x in ((0, 0), (1, cx - 1)):
            pl.when(there[0][side])(lambda: copy(0, side, xsrc, False).wait_recv())
            theirs = [xr[xsrc, side, w] + owed[side, w] for w in range(NV)]
            added = across_face(theirs, side, by_slope, by_side)
            for v in range(NV):
                U[dst, v, x, PAD:PAD + cz, :] = xs[xdst, side, v] + added[v]

    height = lax.broadcasted_iota(jnp.int32, (cr, slots), 0)
    rows_of = lax.broadcasted_iota(jnp.int32, (cx * cz, slots), 0)

    def sample(step):
        spot = line[...]
        chosen_lane = jnp.where(height == spot % cr, 1.0, 0.0).astype(jnp.bfloat16)
        for j in range(4):
            tile = jnp.concatenate([U[0, j, x, PAD:PAD + cz, :] for x in range(cx)], axis=0)
            if j == 0:
                tile = tile + jnp.concatenate([U[0, 4, x, PAD:PAD + cz, :] for x in range(cx)], axis=0)
            picked = split_dot(tile, chosen_lane)
            picked = jnp.where(rows_of == spot // cr, picked, 0.0)
            picked = jnp.sum(picked, axis=0, keepdims=True)
            samples[step, j:j + 1, :] = picked

    loads[0].wait()
    pl.semaphore_wait(barrier, nx - 1 + plane - 1)
    for side in range(2):
        xs[0, side] = U[0, :, (cx - 1) * side, PAD:PAD + cz, :]
    start_x(0)

    def body(k, carry):
        slot = lax.rem(k, 3)
        start_zr(slot)

        @pl.when(k == 0)
        def _():
            prepare()
            for x in loads[3:]:
                x.wait()
            lax.fori_loop(0, observers // 32, geometry, 0)
            spectra()

        for step in range(STEPS - 1):
            @pl.when(k == 3 * step + 3)
            def _():
                sample(step)
                grow(step)

        fill(k)
        stage(k)
        wait_sent(k)
        return carry

    lax.fori_loop(0, stages, body, 0)
    result = pltpu.make_async_copy(U.at[0, :, :, pl.ds(PAD, cz), :], field, load_sem.at[0])
    result.start()
    sample(STEPS - 1)

    def first(d):
        to = lax.rem(seat + d, plane)
        return pltpu.make_async_remote_copy(
            src_ref=value.at[pl.ds(pl.multiple_of(to * nx, nx), nx)],
            dst_ref=got.at[d - 1], send_sem=send1.at[0], recv_sem=recv1.at[0],
            device_id=across(d), device_id_type=MESH,
        )

    def second(d):
        to = lax.rem(a + d, nx)
        return pltpu.make_async_remote_copy(
            src_ref=rows.at[to], dst_ref=last.at[d - 1],
            send_sem=send2.at[d - 1], recv_sem=recv2.at[d - 1],
            device_id=along(d), device_id_type=MESH,
        )

    def chunk(n, carry):
        pair = (2 * n + 1, 2 * n + 2)
        for d in pair:
            last_tile(lax.rem(seat + d, plane), 0)
        first(pair[0]).start()
        pl.when(pair[1] < plane)(lambda: first(pair[1]).start())
        return carry

    lax.fori_loop(0, plane // 2, chunk, 0)
    total = value[pl.ds(pl.multiple_of(seat * nx, nx), nx)]
    everything = pltpu.make_async_remote_copy(
        src_ref=got, dst_ref=got, send_sem=send1.at[0], recv_sem=recv1.at[0],
        device_id=across(1), device_id_type=MESH,
    )
    everything.wait_recv()
    total = total + jnp.sum(got[...], axis=0)
    rows[...] = total[:, None, :]
    for d in range(1, nx):
        second(d).start()
    for d in range(1, nx):
        second(d).wait_recv()
    total = rows[a] + jnp.sum(last[...], axis=0)
    spectrum = total * turns[9:10, :]
    for n, shift in enumerate((96, 64, 32)):
        spectrum = spectrum + pltpu.roll(total, shift, 1) * turns[10 + n:11 + n, :]
    out[...] = spectrum[:, :2 * FREQ]
    everything.wait_send()
    for d in range(1, nx):
        second(d).wait_send()
    result.wait()


def finish_kernel(field_in, spectrum_in, field, spectrum, held, line, sem):
    pairs = [(field_in.at[v], held.at[v], field.at[v]) for v in range(NV)]
    pairs.append((spectrum_in, line, spectrum))
    into = [pltpu.make_async_copy(p[0], p[1], sem.at[0, n]) for n, p in enumerate(pairs)]
    back = [pltpu.make_async_copy(p[1], p[2], sem.at[1, n]) for n, p in enumerate(pairs)]
    for x in into:
        x.start()
    for x, y in zip(into, back):
        x.wait()
        y.start()
    for y in back:
        y.wait()


def finish(field, spectrum):
    hbm = pl.BlockSpec(memory_space=pltpu.HBM)
    return pl.pallas_call(
        finish_kernel,
        out_shape=(
            jax.ShapeDtypeStruct(field.shape, F32),
            jax.ShapeDtypeStruct(spectrum.shape, F32),
        ),
        in_specs=[hbm, hbm],
        out_specs=(hbm, hbm),
        scratch_shapes=[
            pltpu.VMEM(field.shape, F32),
            pltpu.VMEM(spectrum.shape, F32),
            pltpu.SemaphoreType.DMA((2, NV + 1)),
        ],
        compiler_params=pltpu.CompilerParams(vmem_limit_bytes=63 << 20),
        name="finish",
    )(field, spectrum)


def solution(mesh):
    counts = tuple(mesh.shape[a] for a in AXES)
    nx, nz, nr = counts
    plane = nz * nr
    assert nx == 8 and plane == 32

    def per_device(flow, jacobian, history, cell, blocks, observers):
        sizes = counts + flow.shape[1:]
        cx, cz, cr = flow.shape[1:]
        slots, times = history.shape[0], history.shape[2]
        seats = observers.shape[1]
        hbm = pl.BlockSpec(memory_space=pltpu.HBM)
        dma = pltpu.SemaphoreType.DMA
        lanes = turn_rows(times)
        field, spectrum = pl.pallas_call(
            functools.partial(whole_kernel, sizes),
            out_shape=(
                jax.ShapeDtypeStruct(flow.shape, F32),
                jax.ShapeDtypeStruct((1, 2 * FREQ), F32),
            ),
            in_specs=[hbm] * 8,
            out_specs=(hbm, pl.BlockSpec(memory_space=pltpu.VMEM)),
            scratch_shapes=[
                pltpu.VMEM((3, NV, cx, cz + 2 * PAD, cr), F32),
                pltpu.VMEM((2, NV, cz, cr), F32),
                pltpu.VMEM(cell.shape, jnp.int32),
                pltpu.VMEM(observers.shape, F32),
                pltpu.SMEM(blocks.shape, jnp.int32),
                pltpu.SMEM((NV, 3, NV), F32),
                pltpu.VMEM((2 * FREQ, times), F32),
                pltpu.VMEM(lanes.shape, F32),
                pltpu.VMEM((NV, slots, times), F32),
                pltpu.VMEM((4, 2, NV, cz, cr), F32),
                pltpu.VMEM((4, 2, NV, cz, cr), F32),
                pltpu.VMEM((3, 2, NV, cx, cr), F32),
                pltpu.VMEM((3, 2, NV, cx, cr), F32),
                pltpu.VMEM((3, cz, cr), F32),
                pltpu.VMEM((3, 2, cz, cr), F32),
                pltpu.VMEM((4, 2 * FREQ, slots), F32),
                pltpu.VMEM((STEPS, 8, slots), F32),
                pltpu.VMEM((8, seats, slots), F32),
                pltpu.VMEM((seats // 8, FREQ, 2, 8, slots), F32),
                pltpu.VMEM((3, seats, 128), F32),
                pltpu.VMEM((1, slots), jnp.int32),
                pltpu.VMEM((seats, 128), F32),
                pltpu.VMEM((plane - 1, nx, 128), F32),
                pltpu.VMEM((nx, 1, 128), F32),
                pltpu.VMEM((nx - 1, 1, 128), F32),
                dma((8,)),
                dma((3, 2, 4)),
                dma((3, 2, 4)),
                dma((1,)),
                dma((1,)),
                dma((nx - 1,)),
                dma((nx - 1,)),
            ],
            compiler_params=pltpu.CompilerParams(
                collective_id=0, has_side_effects=True, vmem_limit_bytes=63 << 20
            ),
            name="whole",
        )(
            flow, cell, observers, blocks, jacobian.transpose(1, 0, 2),
            jnp.asarray(fourier_table(times)), jnp.asarray(lanes), history.transpose(1, 0, 2),
        )
        return finish(field, spectrum)

    return jax.shard_map(
        per_device,
        mesh=mesh,
        in_specs=(
            P(None, "gx", "gz", "row"),
            P(),
            P(AXES, None, None),
            P(AXES, None),
            P("row", ("gx", "gz")),
            P(),
        ),
        out_specs=(P(None, "gx", "gz", "row"), P(AXES, None)),
        check_vma=False,
    )
```
